128 devices in a mesh: facet: 8 (over y, core), sub: 16 (over x, z).
Axes of the slice: x: 4, y: 4, z: 4, core: 2. Of those that a mesh axis runs over, the one named last changes fastest.
Arguments:
- facets: bfloat16 [8, 1024, 1024], P('facet'), may hold values from -6 to 6
- tapers: float32 [2, 1024], replicated, may hold values from 0.2 to 1
- row_offsets: int32 [8], replicated, may hold values from 0 to 7679
- col_offsets: int32 [16], P('sub'), may hold values from 0 to 7679
- block_subgrid: int32 [128, 1], P(('facet', 'sub')), may hold values from 0 to 15; in each aligned block of 16 rows (0 to 15, 16 to 31, ...) at most 2 rows name the same one
- vis_count: int32 [128], P(('facet', 'sub')), may hold values from 1 to 1024, 81920 in all
- positions: float32 [128, 2, 1024], P(('facet', 'sub')), may hold values from -0.5 to 0.5
- observed: float32 [128, 2, 1024], P(('facet', 'sub')), may hold values from -6 to 6
Outputs:
- residual_vis: float32 [128, 2, 1024], P(('facet', 'sub'))
- residual_subgrids: float32 [8, 16, 512, 1024], P('facet', 'sub')
The draws below stay inside these ranges and needn't reach their ends.
Inputs may be any that keep to these rules, and one draw needn't show every extreme that they name: `block_subgrid`: among the blocks of one index of facet (aligned blocks of 16 rows), at most 2 name the same column, and in every draw some column is named by exactly 2 of them. `vis_count`: the largest count over all blocks is exactly 1024.
All inputs are finite; a program needn't handle non-finite values.
Results may differ from the reference program's by a relative error of at most 0.013.
Values may be sent and summed in bfloat16 or wider, within the bound.
A program may use at most 64 MiB of HBM per device.

```python
import math
import jax
import jax.numpy as jnp
import numpy as np
from jax import lax

M = 512
FS = 1024
NIMG = 8192
STRIDE = 8
ROWS = 1024
MOST = 2
NBLK = 128
N_FACET = 8
N_SUB = 16


def set_ends(entries, own_key, smallest, largest):
    shape = entries.shape
    spot = [jax.random.randint(jax.random.fold_in(own_key, axis), (), 0, shape[axis]) for axis in range(len(shape))]
    entries = entries.at[tuple(spot)].set(smallest)
    longest = shape.index(max(shape))
    spot[longest] = (spot[longest] + 1) % shape[longest]
    return entries.at[tuple(spot)].set(largest)


def level_of(key, dims, cuts, smallest, top_value):
    def one(dim, shards_of):
        draws = jax.random.uniform(jax.random.fold_in(jax.random.fold_in(key, 6), dim), (shards_of,), jnp.float32, smallest / len(cuts), top_value / len(cuts))
        return jnp.repeat(jnp.exp(draws), dims[dim] // shards_of).reshape((-1,) + (1,) * (len(dims) - dim - 1))

    loudness = one(*cuts[0])
    for cut in cuts[1:]:
        loudness = loudness * one(*cut)
    return loudness


def split_up(number_of, total, most, slope):
    weights = [(1 << 20) // math.isqrt(grade ** slope) + 1 for grade in range(2, number_of + 1)]
    rest, holding = total - most - (number_of - 1), [1] * (number_of - 1)
    while rest > 0:
        free = [i for i in range(number_of - 1) if holding[i] < most]
        whole, remaining = sum([weights[i] for i in free]), rest
        for i in free:
            more = min(most - holding[i], max(1, remaining * weights[i] // whole), rest)
            holding[i] = holding[i] + more
            rest = rest - more
    return np.array([most] + holding)


def uneven_parts(stream_key, amount, total, limit, lean):
    if amount == 2:
        one = jax.random.randint(stream_key, (), max(1, total - limit), min(limit, total - 1) + 1)
        return jnp.stack([one, total - one])
    sizes = jnp.asarray(split_up(amount, total, limit, lean), jnp.int32)
    twos = (amount - 1) // 2
    giver, sink = sizes[1:1 + 2 * twos:2], sizes[2:2 + 2 * twos:2]
    margin = jnp.minimum(giver - 1, limit - sink)
    moved = jax.random.randint(jax.random.fold_in(stream_key, 1), (twos,), 0, 1 << 20) % (margin + 1)
    sizes = sizes.at[1:1 + 2 * twos:2].set(giver - moved).at[2:2 + 2 * twos:2].set(sink + moved)
    return sizes[jax.random.permutation(jax.random.fold_in(stream_key, 2), amount)]


def shared_out(stream_key, own, number, rows, number_of, top, most, lean):
    sequence = jax.random.permutation(stream_key, number_of)
    crowded, common = load_shares(number_of, rows * top, most, lean, True), load_shares(number_of, rows * top, most, lean, False)
    places = jnp.arange(number_of)

    def named(tallies, offset_by):
        used = int((tallies > 0).sum())
        fixed = max(1, used // 4)
        moved = fixed + (places - fixed + offset_by * (used - fixed)) % max(1, number_of - fixed)
        return jnp.zeros((number_of,), jnp.int32).at[sequence[jnp.where(places < fixed, places, moved)]].set(jnp.asarray(tallies, jnp.int32))

    tallies = jnp.where(number % 4 == 0, named(crowded, number // 4), named(common, number - number // 4 - 1))
    mixed = jax.random.permutation(jax.random.fold_in(own, 3), number_of)
    source_of, sink = mixed[0:number_of // 2 * 2:2], mixed[1:number_of // 2 * 2:2]
    margin = jnp.minimum(tallies[source_of] - 1, most - tallies[sink]) // 2
    margin = jnp.where((source_of == sequence[0]) | (sink == sequence[0]) | (tallies[sink] == 0), 0, jnp.maximum(margin, 0))
    moved = jax.random.randint(jax.random.fold_in(own, 4), (number_of // 2,), 0, 1 << 20) % (margin + 1)
    tallies = tallies.at[source_of].add(-moved).at[sink].add(moved)
    members = jnp.searchsorted(jnp.cumsum(tallies), jnp.arange(rows * top), side="right").astype(jnp.int32)
    listing = members.reshape(top, rows).T
    listing = listing[jax.random.permutation(jax.random.fold_in(own, 1), rows)]
    offset_by = jax.random.randint(jax.random.fold_in(own, 2), (rows, 1), 0, top)
    return jnp.take_along_axis(listing, (jnp.arange(top)[None, :] + offset_by) % top, axis=1)


def load_shares(number_of, total, bound, slope, full):
    loads = [(1 << 20) // math.isqrt(standing ** slope) + 1 for standing in range(1, number_of + 1)]
    largest = bound if full else min(bound, max(-(-total // number_of), total * loads[0] // sum(loads)))
    least = 1 if total - largest >= number_of - 1 else 0
    holding, surplus = [largest] + [least] * (number_of - 1), total - largest - least * (number_of - 1)
    while surplus > 0:
        candidates = [i for i in range(1, number_of) if holding[i] < largest] or [i for i in range(1, number_of) if holding[i] < bound]
        whole, remaining = sum([loads[i] for i in candidates]), surplus
        for i in candidates:
            addition = min(bound - holding[i], max(1, remaining * loads[i] // whole), surplus)
            holding[i] = holding[i] + addition
            surplus = surplus - addition
    return np.array(holding)


def noise(own_key, extent, width, bound, cuts=(), held_as=jnp.bfloat16):
    gain = level_of(own_key, extent, cuts, -0.22, 0.18) if cuts else 1.0
    entries = jax.random.normal(own_key, extent, jnp.float32) * width * gain
    return jnp.minimum(jnp.maximum(entries, -bound), bound).astype(held_as)


def setup_inputs(seed: int = 0) -> dict:
    splits = jax.random.split(jax.random.key(seed), 9)
    facets = noise(splits[0], (N_FACET, FS, FS), 1.0, 6.0, ((0, 8),))
    tapers = jnp.clip(jax.random.uniform(splits[1], (2, FS), jnp.float32, 0.2, 1.0), 0.2, 1.0)
    row_offsets = set_ends(jax.random.randint(splits[2], (N_FACET,), 0, NIMG - M), jax.random.fold_in(splits[2], 1), 0, (NIMG - M) - 1).astype(jnp.int32)
    col_offsets = set_ends(jax.random.randint(splits[3], (N_SUB,), 0, NIMG - M), jax.random.fold_in(splits[3], 1), 0, (NIMG - M) - 1).astype(jnp.int32)
    block_subgrid_keys = jax.random.split(jax.random.fold_in(splits[4], 1), NBLK // N_SUB)
    block_subgrid_turns = jax.random.permutation(jax.random.fold_in(splits[4], 3), NBLK // N_SUB)
    block_subgrid = jax.vmap(lambda own, number: shared_out(jax.random.fold_in(splits[4], 2), own, number, N_SUB, N_SUB, 1, MOST, 2))(block_subgrid_keys, block_subgrid_turns).reshape((NBLK, 1))
    vis_count = uneven_parts(splits[5], NBLK, NBLK * ROWS * 5 // 8, ROWS, 1).astype(jnp.int32)
    positions = jnp.clip(jax.random.uniform(splits[6], (NBLK, 2, ROWS), jnp.float32, -0.5, 0.5) * level_of(splits[6], (NBLK, 2, ROWS), ((0, 128),), -0.4, 0.0), -0.5, 0.5)
    observed = noise(splits[7], (NBLK, 2, ROWS), 1.0, 6.0, ((0, 128),), jnp.float32)
    return {"facets": facets, "tapers": tapers, "row_offsets": row_offsets, "col_offsets": col_offsets, "block_subgrid": block_subgrid, "vis_count": vis_count, "positions": positions, "observed": observed}


TWO_PI = 2.0 * math.pi

def rounded(values):
    return lax.optimization_barrier(values.astype(jnp.bfloat16)).astype(jnp.float32)

def column_table(offset):
    frequency = (offset + STRIDE * jnp.arange(M, dtype=jnp.int32)) % NIMG
    coords = jnp.arange(FS, dtype=jnp.int32)
    residue = coords[:, None] * frequency[None, :] % NIMG
    angles = residue.astype(jnp.float32) * (TWO_PI / NIMG)
    return rounded(jnp.concatenate([jnp.cos(angles), -jnp.sin(angles)], axis=1))

def row_tables(offset):
    frequency = (offset + STRIDE * jnp.arange(M, dtype=jnp.int32)) % NIMG
    coords = jnp.arange(N_FACET, dtype=jnp.int32)[:, None] * FS + jnp.arange(FS, dtype=jnp.int32)[None, :]
    residue = frequency[None, :, None] * coords[:, None, :] % NIMG
    angles = residue.astype(jnp.float32) * (TWO_PI / NIMG)
    return rounded(jnp.concatenate([jnp.cos(angles), -jnp.sin(angles)], axis=2))

def complex_block(matrix):
    half_width = matrix.shape[-1] // 2
    real_part = matrix[..., :half_width]
    imaginary = matrix[..., half_width:]
    lower = jnp.concatenate([-imaginary, real_part], axis=-1)
    return jnp.concatenate([matrix, lower], axis=-2)

def phasors(coords):
    centered = jnp.arange(M).astype(jnp.float32) - M // 2
    angles = TWO_PI * coords[:, None] * centered[None, :]
    return (jnp.cos(angles), jnp.sin(angles))

def degrid(subgrid, position, observed, live_count):
    row_total = position.shape[1]
    first_cosine, first_sine = phasors(position[0])
    second_cosine, second_sine = phasors(position[1])
    u_table = rounded(jnp.concatenate([first_cosine, first_sine], axis=1))
    lifted = jnp.dot(u_table, complex_block(subgrid.astype(jnp.float32)))
    lifted_real = lifted[:, :M]
    lifted_imaginary = lifted[:, M:]
    model_real = lax.optimization_barrier(jnp.sum(lifted_real * second_cosine - lifted_imaginary * second_sine, axis=1)) / M
    model_imaginary = lax.optimization_barrier(jnp.sum(lifted_real * second_sine + lifted_imaginary * second_cosine, axis=1)) / M
    live_rows = jnp.arange(row_total, dtype=jnp.int32) < live_count
    residual_real = jnp.where(live_rows, observed[0] - model_real, 0.0)
    residual_imaginary = jnp.where(live_rows, observed[1] - model_imaginary, 0.0)
    weight_real = residual_real[:, None] * second_cosine + residual_imaginary[:, None] * second_sine
    weight_imaginary = residual_imaginary[:, None] * second_cosine - residual_real[:, None] * second_sine
    weights = rounded(jnp.concatenate([weight_real, weight_imaginary], axis=1))
    outer_sums = jnp.dot(u_table.T, weights)
    partial_real = outer_sums[:M, :M] + outer_sums[M:, M:]
    partial_imaginary = outer_sums[:M, M:] - outer_sums[M:, :M]
    partial_value = jnp.concatenate([partial_real, partial_imaginary], axis=1) * (1.0 / math.sqrt(row_total))
    return (jnp.stack([residual_real, residual_imaginary]), rounded(partial_value))

def reference(facets, tapers, row_offsets, col_offsets, block_subgrid, vis_count, positions, observed):
    tapered = rounded(facets.astype(jnp.float32) * tapers[0][None, :, None] * tapers[1][None, None, :])

    def one_column(col_offset):
        table = column_table(col_offset)
        spectra = rounded(jnp.einsum('fxy,yl->fxl', tapered, table))
        blocks = complex_block(spectra)

        def one_row(row_offset):
            phase_rows = row_tables(row_offset)
            pieces = jnp.einsum('fkx,fxl->fkl', phase_rows, blocks) * (1.0 / FS)
            return rounded(lax.optimization_barrier(jnp.sum(rounded(pieces), axis=0)))
        return lax.map(one_row, row_offsets)
    grids = lax.map(one_column, col_offsets)

    def one_block(accumulated, block_index):
        facet_row = block_index // N_SUB
        target = block_subgrid[block_index, 0]
        subgrid = grids[target, facet_row]
        residual_rows, partial_value = degrid(subgrid, positions[block_index], observed[block_index], vis_count[block_index])
        owner_slot = facet_row * N_SUB + target
        accumulated = accumulated.at[owner_slot].add(partial_value)
        return (accumulated, residual_rows)
    start_sums = jnp.zeros((N_FACET * N_SUB, M, 2 * M), jnp.float32)
    accumulated, residual_rows = lax.scan(one_block, start_sums, jnp.arange(N_FACET * N_SUB, dtype=jnp.int32))
    return (residual_rows, accumulated.reshape(N_FACET, N_SUB, M, 2 * M))
```

```python
import functools
import math

import jax
import jax.numpy as jnp
from jax import lax
from jax.experimental import pallas as pl
from jax.experimental.pallas import tpu as pltpu
from jax.sharding import PartitionSpec as P

M = 512
HALF = 256
FS = 1024
NIMG = 8192
ROWS = 1024
NF = 8
NS = 16
MESH = pl.DeviceIdType.MESH
F32 = jnp.float32
BF16 = jnp.bfloat16
I32 = jnp.int32


def turn(t):
    u = (t - jnp.round(t)) * math.pi
    v = u * u
    s = 1.0 / 6227020800.0
    for c in (-1.0 / 39916800.0, 1.0 / 362880.0, -1.0 / 5040.0, 1.0 / 120.0, -1.0 / 6.0, 1.0):
        s = s * v + c
    s = s * u
    k = 1.0 / 479001600.0
    for c in (-1.0 / 3628800.0, 1.0 / 40320.0, -1.0 / 720.0, 1.0 / 24.0, -0.5, 1.0):
        k = k * v + c
    return 1.0 - 2.0 * s * s, 2.0 * s * k


def grow(base, coarse, steps, put):
    bc, bs = base

    def step(q, carry):
        cc, cs = coarse(q)
        put(q, bc * cc - bs * cs, bs * cc + bc * cs)
        return carry

    lax.fori_loop(0, steps, step, 0)


def iota(shape, dim):
    return lax.broadcasted_iota(I32, shape, dim)


def half_steps(p, n, m_ref):
    shape = (16, n)
    rows = iota(shape, 0).astype(F32)
    m_ref[0], m_ref[1] = turn(p * (rows + 0.5))
    m_ref[2], m_ref[3] = turn(p * (rows * 16.0))


def basis_into(m_ref, lanes, put):
    for at, width in lanes:
        base = (m_ref[0, :, pl.ds(at, width)], m_ref[1, :, pl.ds(at, width)])

        def coarse(q, at=at, width=width):
            return m_ref[2, pl.ds(q, 1), pl.ds(at, width)], m_ref[3, pl.ds(q, 1), pl.ds(at, width)]

        def put_here(q, c, s, at=at, width=width):
            put(pl.multiple_of(q * 16, 16), at, width, c, s)

        grow(base, coarse, 16, put_here)


def front(
    facets, tapers, row_off, col_off, target, count, pos, obs,
    res_all, pos_all, meta_all,
    fac, tt, facs, bt, zs, ptn, qg, qm, ec, es, ub, vb, hs, small, res_src, meta_src,
    load_sem, a_send, a_recv, d_send, d_recv, b_send, b_recv, m_send, m_recv, p_send, p_recv, c_send, c_recv,
):
    f = lax.axis_index("facet")
    j = lax.axis_index("sub")
    core = lax.rem(f, 2)
    x, z = j // 4, lax.rem(j, 4)
    pair, odd = j // 2, lax.rem(j, 2)
    at128 = pl.multiple_of(pair * 128, 128)

    load = pltpu.make_async_copy(facets.at[0, :, pl.ds(at128, 128)], fac, load_sem)
    load.start()

    barrier = pltpu.get_barrier_semaphore()
    for d in range(1, NF):
        pl.semaphore_signal(barrier, inc=1, device_id={"facet": lax.rem(f + d, NF)}, device_id_type=MESH)
    for d in range(1, NS):
        pl.semaphore_signal(barrier, inc=1, device_id={"sub": lax.rem(j + d, NS)}, device_id_type=MESH)

    rows8 = iota((8, 128), 0)
    meta_src[...] = jnp.where(rows8 == 0, col_off[0], jnp.where(rows8 == 1, target[0, 0], count[0]))
    meta_all[j] = meta_src[...]
    pos_all[j] = pos[0]

    load.wait()
    by_column = fac[...].astype(F32) * tapers[1:2, pl.ds(at128, 128)]
    turned = (by_column.T * tapers[0:1, :]).astype(BF16)
    for g in range(4):
        tt[g] = turned[g * 32 : g * 32 + 32]
    facs[f] = tt[2 * odd + core]

    pl.semaphore_wait(barrier, NF - 1 + NS - 1)
    a_copies, m_copies = [], []
    for d in range(1, NF):
        peer = lax.rem(f + d, NF)
        copy = pltpu.make_async_remote_copy(
            src_ref=tt.at[2 * odd + lax.rem(peer, 2)], dst_ref=facs.at[f],
            send_sem=a_send.at[d - 1], recv_sem=a_recv.at[d - 1],
            device_id={"facet": peer}, device_id_type=MESH,
        )
        copy.start()
        a_copies.append(copy)
    for d in range(1, NS):
        peer = lax.rem(j + d, NS)
        for src, dst, ss, rs in ((meta_src, meta_all, m_send, m_recv), (pos.at[0], pos_all, p_send, p_recv)):
            copy = pltpu.make_async_remote_copy(
                src_ref=src, dst_ref=dst.at[j], send_sem=ss.at[d - 1], recv_sem=rs.at[d - 1],
                device_id={"sub": peer}, device_id_type=MESH,
            )
            copy.start()
            m_copies.append(copy)

    lane = iota((16, FS), 1)
    row = iota((16, FS), 0)
    small[0], small[1] = turn((((2 * row + 1) * lane) & 2047).astype(F32) * (1.0 / 2048))
    small[2], small[3] = turn(((32 * row * lane) & 2047).astype(F32) * (1.0 / 2048))

    def put_bt(at, lane_at, width, c, s):
        bt[pl.ds(at, 16), pl.ds(lane_at, width)] = c.astype(BF16)
        bt[pl.ds(at + HALF, 16), pl.ds(lane_at, width)] = s.astype(BF16)

    lanes4 = [(0, 256), (256, 256), (512, 256), (768, 256)]
    basis_into(small, lanes4, put_bt)

    phases = []
    rows_f = iota((NF, FS), 0)
    lane_f = iota((NF, FS), 1)
    for aa in range(2):
        off = row_off[2 * (f // 2) + aa]
        r = (off * (rows_f * FS + lane_f) + 2044 * lane_f) & (NIMG - 1)
        c, s = turn(r.astype(F32) * (1.0 / NIMG))
        phases.append((c, -s))

    for d in range(1, NF):
        a_copies[d - 1].wait_recv()
    for at, width in lanes4:
        sums = [jnp.zeros((32, width), F32) for _ in range(4)]
        for g in range(NF):
            t = facs[g, :, at : at + width].astype(F32)
            for aa in range(2):
                sums[2 * aa] = sums[2 * aa] + t * phases[aa][0][g : g + 1, at : at + width]
                sums[2 * aa + 1] = sums[2 * aa + 1] + t * phases[aa][1][g : g + 1, at : at + width]
        for i in range(4):
            zs[i * 32 : i * 32 + 32, at : at + width] = sums[i].astype(BF16)
    turned_rows = lax.dot_general(
        zs[...], bt[...], (((1,), (1,)), ((), ())), preferred_element_type=F32
    ).astype(BF16)
    q_rows = [[jnp.concatenate([
        turned_rows[aa * 64 : aa * 64 + 32, hf * HALF : hf * HALF + HALF],
        turned_rows[aa * 64 + 32 : aa * 64 + 64, hf * HALF : hf * HALF + HALF],
    ], axis=1) for hf in range(2)] for aa in range(2)]
    mine_first = core == 0
    for hf in range(2):
        qg[hf, j, core] = jnp.where(mine_first, q_rows[0][hf], q_rows[1][hf])
        ptn[hf] = jnp.where(mine_first, q_rows[1][hf], q_rows[0][hf])
    d_copies = []
    for hf in range(2):
        copy = pltpu.make_async_remote_copy(
            src_ref=ptn.at[hf], dst_ref=qg.at[hf, j, core],
            send_sem=d_send.at[hf], recv_sem=d_recv.at[hf],
            device_id={"facet": f + 1 - 2 * core}, device_id_type=MESH,
        )
        copy.start()
        d_copies.append(copy)

    def place(hf, dp, dq):
        dx, dz = (dq, dp) if hf == 0 else (dp, dq)
        return 4 * lax.rem(x + dx % 4, 4) + lax.rem(z + dz % 4, 4)

    b_copies = []

    def send(hf, dp, dq, rh, ep, eq):
        copy = pltpu.make_async_remote_copy(
            src_ref=qg.at[hf, place(hf, dp, dq), rh], dst_ref=qg.at[hf, place(hf, dp, dq), rh],
            send_sem=b_send.at[len(b_copies)],
            recv_sem=b_recv.at[hf, (dq - eq) % 4, (dp - ep) % 4, rh],
            device_id={"sub": place(hf, ep, eq)}, device_id_type=MESH,
        )
        copy.start()
        b_copies.append(copy)

    def arrived(hf, dp, dq, rh):
        pltpu.make_async_remote_copy(
            src_ref=qg.at[hf, place(hf, dp, dq), rh], dst_ref=qg.at[hf, place(hf, dp, dq), rh],
            send_sem=b_send.at[0], recv_sem=b_recv.at[hf, dq % 4, dp % 4, rh],
            device_id={"sub": j}, device_id_type=MESH,
        ).wait_recv()

    four = ((0, 1), (0, -1), (1, 0), (-1, 0))
    for hf in range(2):
        for ep, eq in four:
            send(hf, 0, 0, core, ep, eq)
    for hf in range(2):
        pltpu.make_async_remote_copy(
            src_ref=ptn.at[hf], dst_ref=qg.at[hf, j, 1 - core],
            send_sem=d_send.at[hf], recv_sem=d_recv.at[hf],
            device_id={"facet": f + 1 - 2 * core}, device_id_type=MESH,
        ).wait_recv()
        for ep, eq in four:
            send(hf, 0, 0, 1 - core, ep, eq)

    half_steps(pos[0, 0:1, :], FS, small)

    def put_ub(at, lane_at, width, c, s):
        ub[pl.ds(at, 16), pl.ds(lane_at, width)] = c.astype(BF16)
        ub[pl.ds(at + HALF, 16), pl.ds(lane_at, width)] = s.astype(BF16)

    basis_into(small, lanes4, put_ub)

    for dp in (-1, 1):
        for rh in range(2):
            for hf in range(2):
                arrived(hf, dp, 0, rh)
                send(hf, dp, 0, rh, 0, 1)
                send(hf, dp, 0, rh, 0, -1)
                if rh == (0 if dp == -1 else 1):
                    send(hf, dp, 0, rh, -dp, 0)

    def across(dp):
        for dq in (-1, 1):
            for rh in range(2):
                for hf in range(2):
                    arrived(hf, dp, dq, rh)
                    if rh == (0 if dq == -1 else 1):
                        send(hf, dp, dq, rh, 0, -dq)

    across(0)
    for rh in range(2):
        for hf in range(2):
            arrived(hf, 2, 0, rh)
            send(hf, 2, 0, rh, 0, 1)
            send(hf, 2, 0, rh, 0, -1)
    across(-1)
    across(1)

    half_steps(pos[0, 1:2, :], FS, small)

    def put_vb(at, lane_at, width, c, s):
        vb[pl.ds(at, 16), pl.ds(lane_at, width)] = c
        vb[pl.ds(at + HALF, 16), pl.ds(lane_at, width)] = s

    basis_into(small, lanes4, put_vb)

    for i in range(len(m_copies)):
        m_copies[i].wait_recv()
    step = meta_all[target[0, 0]][0:1, :] + 2044
    rows128 = iota((16, 128), 0)
    base_c, base_s = turn(((step * rows128) & (NIMG - 1)).astype(F32) * (1.0 / NIMG))
    for q in range(64):
        cc, cs = turn(((step * (16 * q)) & (NIMG - 1)).astype(F32) * (1.0 / NIMG))
        ec[q * 16 : q * 16 + 16] = base_c * cc - base_s * cs
        es[q * 16 : q * 16 + 16] = -(base_s * cc + base_c * cs)

    across(2)
    for dp in (0, -1, 1, 2):
        for rh in range(2):
            for hf in range(2):
                arrived(hf, dp, 2, rh)

    def modulate(i, carry):
        at = pl.multiple_of(i * 32, 32)
        c, s = ec[pl.ds(at, 32)], es[pl.ds(at, 32)]
        for hf in range(2):
            for k in range(2):
                re = qg[hf, i // 2, lax.rem(i, 2), :, k * 128 : k * 128 + 128].astype(F32)
                im = qg[hf, i // 2, lax.rem(i, 2), :, 256 + k * 128 : 384 + k * 128].astype(F32)
                qm[hf, pl.ds(at, 32), k * 128 : k * 128 + 128] = (re * c - im * s).astype(BF16)
                qm[hf, pl.ds(at, 32), 256 + k * 128 : 384 + k * 128] = (re * s + im * c).astype(BF16)
        return carry

    lax.fori_loop(0, 32, modulate, 0)
    for hf in range(2):
        both = jnp.dot(bt[...], qm[hf], preferred_element_type=F32).astype(BF16)
        hs[0:M, hf * HALF : hf * HALF + HALF] = both[:, 0:HALF]
        hs[M : 2 * M, hf * HALF : hf * HALF + HALF] = both[:, HALF:M]

    live_count = count[0]

    def degrid(i, carry):
        at = pl.multiple_of(i * 256, 256)
        lifted = jnp.dot(hs[...], ub[:, pl.ds(at, 256)], preferred_element_type=F32)
        v = vb[:, pl.ds(at, 256)]
        sum_re = jnp.sum(lifted[0:M] * v, axis=0, keepdims=True)
        sum_im = jnp.sum(lifted[M : 2 * M] * v, axis=0, keepdims=True)
        c, s = turn((pos[0, 0:1, pl.ds(at, 256)] + pos[0, 1:2, pl.ds(at, 256)]) * 0.5)
        scale = 4.0 / (M * FS)
        live = iota((1, 256), 1) + at < live_count
        re = obs[0, 0:1, pl.ds(at, 256)] - (sum_re * c + sum_im * s) * scale
        im = obs[0, 1:2, pl.ds(at, 256)] - (sum_im * c - sum_re * s) * scale
        res_src[0:1, pl.ds(at, 256)] = jnp.where(live, re, 0.0)
        res_src[1:2, pl.ds(at, 256)] = jnp.where(live, im, 0.0)
        return carry

    lax.fori_loop(0, 4, degrid, 0)

    c_copies = []
    for d in range(1, NS):
        copy = pltpu.make_async_remote_copy(
            src_ref=res_src, dst_ref=res_all.at[j], send_sem=c_send.at[d - 1], recv_sem=c_recv.at[d - 1],
            device_id={"sub": lax.rem(j + d, NS)}, device_id_type=MESH,
        )
        copy.start()
        c_copies.append(copy)
    res_all[j] = res_src[...]
    for copy in a_copies + m_copies + d_copies + b_copies:
        copy.wait_send()
    for copy in c_copies:
        copy.wait()


CHUNK = 256


def back(meta, res_all, pos_all, res_out, grid_out, total, ubc, wc, mu, mv, rot):
    j = lax.axis_index("sub")
    res_out[0] = res_all[j]
    total[...] = jnp.zeros_like(total)

    def one(b, carry):
        @pl.when(meta[b, 1, 0] == j)
        def _():
            p = pos_all[b]
            half_steps(p[0:1, :], ROWS, mu)
            half_steps(p[1:2, :], ROWS, mv)
            c, s = turn((p[0:1, :] + p[1:2, :]) * 0.5)
            r = res_all[b]
            rot[0:1, :] = r[0:1, :] * c - r[1:2, :] * s
            rot[1:2, :] = r[0:1, :] * s + r[1:2, :] * c

            def chunk(i, carry):
                at = pl.multiple_of(i * CHUNK, CHUNK)

                def put_u(to, lane_at, width, c, s):
                    ubc[pl.ds(to, 16), :] = c.astype(BF16)
                    ubc[pl.ds(to + HALF, 16), :] = s.astype(BF16)

                re, im = rot[0:1, pl.ds(at, CHUNK)], rot[1:2, pl.ds(at, CHUNK)]

                def put_w(to, lane_at, width, c, s):
                    wc[pl.ds(to, 16), :] = (c * re).astype(BF16)
                    wc[pl.ds(to + HALF, 16), :] = (s * re).astype(BF16)
                    wc[pl.ds(to + M, 16), :] = (c * im).astype(BF16)
                    wc[pl.ds(to + M + HALF, 16), :] = (s * im).astype(BF16)

                basis_into(mu, [(at, CHUNK)], put_u)
                basis_into(mv, [(at, CHUNK)], put_w)
                total[...] += lax.dot_general(
                    ubc[...], wc[...], (((1,), (1,)), ((), ())), preferred_element_type=F32
                )
                return carry

            lax.fori_loop(0, (meta[b, 2, 0] + CHUNK - 1) // CHUNK, chunk, 0)

        return carry

    lax.fori_loop(0, NS, one, 0)

    scale = 1.0 / math.sqrt(ROWS)
    flip = jnp.where(iota((HALF, HALF), 0) + iota((HALF, HALF), 1) == HALF - 1, 1.0, 0.0).astype(BF16)

    def flip_columns(a):
        return jnp.dot(a.astype(BF16), flip, preferred_element_type=F32)

    def quarter(k, l, im):
        return total[k * HALF : k * HALF + HALF, im * M + l * HALF : im * M + l * HALF + HALF]

    for im in range(2):
        sign = 1.0 if im == 0 else -1.0
        cc, ss = quarter(0, 0, im), quarter(1, 1, im)
        cs, sc = quarter(0, 1, 1 - im), quarter(1, 0, 1 - im)
        even, both = (cc - ss) * scale, (cc + ss) * scale
        y, w = (cs + sc) * (scale * sign), (cs - sc) * (scale * sign)
        grid_out[0, 0, HALF:M, im * M + HALF : im * M + M] = even + y
        grid_out[0, 0, HALF:M, im * M : im * M + HALF] = flip_columns(both - w)
        top_right = (both + w).astype(BF16)
        top_left = flip_columns(even - y).astype(BF16)
        grid_out[0, 0, 0:HALF, im * M + HALF : im * M + M] = jnp.dot(flip, top_right, preferred_element_type=F32)
        grid_out[0, 0, 0:HALF, im * M : im * M + HALF] = jnp.dot(flip, top_left, preferred_element_type=F32)


def per_device(facets, tapers, row_offsets, col_offsets, block_subgrid, vis_count, positions, observed):
    vmem = pl.BlockSpec(memory_space=pltpu.VMEM)
    smem = pl.BlockSpec(memory_space=pltpu.SMEM)
    dma = pltpu.SemaphoreType.DMA
    res_all, pos_all, meta_all = pl.pallas_call(
        front,
        out_shape=(
            jax.ShapeDtypeStruct((NS, 2, ROWS), F32),
            jax.ShapeDtypeStruct((NS, 2, ROWS), F32),
            jax.ShapeDtypeStruct((NS, 8, 128), I32),
        ),
        in_specs=[pl.BlockSpec(memory_space=pl.ANY), vmem, smem, smem, smem, smem, vmem, vmem],
        out_specs=(vmem, vmem, vmem),
        scratch_shapes=[
            pltpu.VMEM((FS, 128), BF16),
            pltpu.VMEM((4, 32, FS), BF16),
            pltpu.VMEM((NF, 32, FS), BF16),
            pltpu.VMEM((M, FS), BF16),
            pltpu.VMEM((128, FS), BF16),
            pltpu.VMEM((2, 32, M), BF16),
            pltpu.VMEM((2, NS, 2, 32, M), BF16),
            pltpu.VMEM((2, FS, M), BF16),
            pltpu.VMEM((FS, 128), F32),
            pltpu.VMEM((FS, 128), F32),
            pltpu.VMEM((M, ROWS), BF16),
            pltpu.VMEM((M, ROWS), F32),
            pltpu.VMEM((2 * M, M), BF16),
            pltpu.VMEM((4, 16, FS), F32),
            pltpu.VMEM((2, ROWS), F32),
            pltpu.VMEM((8, 128), I32),
            dma(()),
            dma((NF - 1,)), dma((NF - 1,)),
            dma((2,)), dma((2,)),
            dma((60,)), dma((2, 4, 4, 2)),
            dma((NS - 1,)), dma((NS - 1,)),
            dma((NS - 1,)), dma((NS - 1,)),
            dma((NS - 1,)), dma((NS - 1,)),
        ],
        compiler_params=pltpu.CompilerParams(collective_id=0, has_side_effects=True),
        name="front",
    )(facets, tapers, row_offsets, col_offsets, block_subgrid, vis_count, positions, observed)
    return pl.pallas_call(
        back,
        out_shape=(
            jax.ShapeDtypeStruct((1, 2, ROWS), F32),
            jax.ShapeDtypeStruct((1, 1, M, 2 * M), F32),
        ),
        in_specs=[smem, vmem, vmem],
        out_specs=(vmem, vmem),
        scratch_shapes=[
            pltpu.VMEM((M, 2 * M), F32),
            pltpu.VMEM((M, CHUNK), BF16),
            pltpu.VMEM((2 * M, CHUNK), BF16),
            pltpu.VMEM((4, 16, ROWS), F32),
            pltpu.VMEM((4, 16, ROWS), F32),
            pltpu.VMEM((2, ROWS), F32),
        ],
        name="back",
    )(meta_all, res_all, pos_all)


def solution(mesh):
    in_specs = (
        P("facet", None, None),
        P(),
        P(),
        P("sub"),
        P(("facet", "sub"), None),
        P(("facet", "sub")),
        P(("facet", "sub"), None, None),
        P(("facet", "sub"), None, None),
    )
    out_specs = (P(("facet", "sub"), None, None), P("facet", "sub", None, None))
    return jax.shard_map(per_device, mesh=mesh, in_specs=in_specs, out_specs=out_specs, check_vma=False)
```

```python
import functools
import math

import jax
import jax.numpy as jnp
from jax import lax
from jax.experimental import pallas as pl
from jax.experimental.pallas import tpu as pltpu
from jax.sharding import PartitionSpec as P

M = 512
HALF = 256
FS = 1024
NIMG = 8192
ROWS = 1024
NF = 8
NS = 16
MESH = pl.DeviceIdType.MESH
F32 = jnp.float32
BF16 = jnp.bfloat16
I32 = jnp.int32


def turn(t):
    u = (t - jnp.round(t)) * math.pi
    v = u * u
    s = 1.0 / 6227020800.0
    for c in (-1.0 / 39916800.0, 1.0 / 362880.0, -1.0 / 5040.0, 1.0 / 120.0, -1.0 / 6.0, 1.0):
        s = s * v + c
    s = s * u
    k = 1.0 / 479001600.0
    for c in (-1.0 / 3628800.0, 1.0 / 40320.0, -1.0 / 720.0, 1.0 / 24.0, -0.5, 1.0):
        k = k * v + c
    return 1.0 - 2.0 * s * s, 2.0 * s * k


def grow(base, coarse, steps, put):
    bc, bs = base

    def step(q, carry):
        cc, cs = coarse(q)
        put(q, bc * cc - bs * cs, bs * cc + bc * cs)
        return carry

    lax.fori_loop(0, steps, step, 0)


def iota(shape, dim):
    return lax.broadcasted_iota(I32, shape, dim)


def half_steps(p, n, m_ref):
    shape = (16, n)
    rows = iota(shape, 0).astype(F32)
    m_ref[0], m_ref[1] = turn(p * (rows + 0.5))
    m_ref[2], m_ref[3] = turn(p * (rows * 16.0))


def basis_into(m_ref, lanes, put):
    for at, width in lanes:
        base = (m_ref[0, :, pl.ds(at, width)], m_ref[1, :, pl.ds(at, width)])

        def coarse(q, at=at, width=width):
            return m_ref[2, pl.ds(q, 1), pl.ds(at, width)], m_ref[3, pl.ds(q, 1), pl.ds(at, width)]

        def put_here(q, c, s, at=at, width=width):
            put(pl.multiple_of(q * 16, 16), at, width, c, s)

        grow(base, coarse, 16, put_here)


def front(
    facets, tapers, row_off, col_off, target, count, pos, obs,
    res_out, grid_out,
    res_all, pos_all, meta_all, fac, tt, facs, bt, zs, ptn, qg, qm, ec, es, ub, vb, hs, hacc, small, meta_src,
    mask, slot_pos, ubo, vbo, wb, total,
    load_sem, a_send, a_recv, d_send, d_recv, b_send, b_recv, m_send, m_recv, p_send, p_recv, c_send, c_recv,
):
    f = lax.axis_index("facet")
    j = lax.axis_index("sub")
    core = lax.rem(f, 2)
    x, z = j // 4, lax.rem(j, 4)
    pair, odd = j // 2, lax.rem(j, 2)
    at128 = pl.multiple_of(pair * 128, 128)

    load = pltpu.make_async_copy(facets.at[0, :, pl.ds(at128, 128)], fac, load_sem)
    load.start()

    barrier = pltpu.get_barrier_semaphore()
    for d in range(1, NF):
        pl.semaphore_signal(barrier, inc=1, device_id={"facet": lax.rem(f + d, NF)}, device_id_type=MESH)
    for d in range(1, NS):
        pl.semaphore_signal(barrier, inc=1, device_id={"sub": lax.rem(j + d, NS)}, device_id_type=MESH)

    rows8 = iota((8, 128), 0)
    meta_src[...] = jnp.where(rows8 == 0, col_off[0], jnp.where(rows8 == 1, target[0, 0], count[0]))
    meta_all[j] = meta_src[...]
    pos_all[j] = pos[0]

    load.wait()
    by_column = fac[...].astype(F32) * tapers[1:2, pl.ds(at128, 128)]
    turned = (by_column.T * tapers[0:1, :]).astype(BF16)
    for g in range(4):
        tt[g] = turned[g * 32 : g * 32 + 32]
    facs[f] = tt[2 * odd + core]

    pl.semaphore_wait(barrier, NF - 1 + NS - 1)
    a_copies, m_copies = [], []
    for d in range(1, NF):
        peer = lax.rem(f + d, NF)
        copy = pltpu.make_async_remote_copy(
            src_ref=tt.at[2 * odd + lax.rem(peer, 2)], dst_ref=facs.at[f],
            send_sem=a_send.at[d - 1], recv_sem=a_recv.at[d - 1],
            device_id={"facet": peer}, device_id_type=MESH,
        )
        copy.start()
        a_copies.append(copy)
    for d in range(1, NS):
        peer = lax.rem(j + d, NS)
        for src, dst, ss, rs in ((meta_src, meta_all, m_send, m_recv), (pos.at[0], pos_all, p_send, p_recv)):
            copy = pltpu.make_async_remote_copy(
                src_ref=src, dst_ref=dst.at[j], send_sem=ss.at[d - 1], recv_sem=rs.at[d - 1],
                device_id={"sub": peer}, device_id_type=MESH,
            )
            copy.start()
            m_copies.append(copy)

    lanes4 = [(0, 256), (256, 256), (512, 256), (768, 256)]

    def table_into(ref, lead, dtype):
        def put(at, lane_at, width, c, s):
            ref[(*lead, pl.ds(at, 16), pl.ds(lane_at, width))] = c.astype(dtype)
            ref[(*lead, pl.ds(at + HALF, 16), pl.ds(lane_at, width))] = s.astype(dtype)

        basis_into(small, lanes4, put)

    lane = iota((16, FS), 1)
    row = iota((16, FS), 0)
    crossed = ((lane >> 6) & 3) * 256 + (lane >> 8) * 64 + (lane & 63)
    for order, at in enumerate((lane, crossed)):
        small[0], small[1] = turn((((2 * row + 1) * at) & 2047).astype(F32) * (1.0 / 2048))
        small[2], small[3] = turn(((32 * row * at) & 2047).astype(F32) * (1.0 / 2048))
        table_into(bt, (order,), BF16)
    half_steps(pos[0, 0:1, :], FS, small)
    table_into(ub, (), BF16)
    half_steps(pos[0, 1:2, :], FS, small)
    table_into(vb, (), F32)

    phases = []
    rows_f = iota((NF, FS), 0)
    lane_f = iota((NF, FS), 1)
    for aa in range(2):
        off = row_off[2 * (f // 2) + aa]
        r = (off * (rows_f * FS + lane_f) + 2044 * lane_f) & (NIMG - 1)
        c, s = turn(r.astype(F32) * (1.0 / NIMG))
        phases.append((c, -s))

    for d in range(1, NF):
        a_copies[d - 1].wait_recv()
    for at, width in lanes4:
        sums = [jnp.zeros((32, width), F32) for _ in range(4)]
        for g in range(NF):
            t = facs[g, :, at : at + width].astype(F32)
            for aa in range(2):
                sums[2 * aa] = sums[2 * aa] + t * phases[aa][0][g : g + 1, at : at + width]
                sums[2 * aa + 1] = sums[2 * aa + 1] + t * phases[aa][1][g : g + 1, at : at + width]
        for i in range(4):
            zs[i * 32 : i * 32 + 32, at : at + width] = sums[i].astype(BF16)
    turned_rows = lax.dot_general(
        zs[...], bt[0], (((1,), (1,)), ((), ())), preferred_element_type=F32
    ).astype(BF16)
    q_rows = [[jnp.concatenate([
        turned_rows[aa * 64 : aa * 64 + 32, hf * HALF : hf * HALF + HALF],
        turned_rows[aa * 64 + 32 : aa * 64 + 64, hf * HALF : hf * HALF + HALF],
    ], axis=1) for hf in range(2)] for aa in range(2)]
    mine_first = core == 0
    for hf in range(2):
        qg[hf, j, core] = jnp.where(mine_first, q_rows[0][hf], q_rows[1][hf])
        ptn[hf] = jnp.where(mine_first, q_rows[1][hf], q_rows[0][hf])
    d_copies = []
    for hf in range(2):
        copy = pltpu.make_async_remote_copy(
            src_ref=ptn.at[hf], dst_ref=qg.at[hf, j, core],
            send_sem=d_send.at[hf], recv_sem=d_recv.at[hf],
            device_id={"facet": f + 1 - 2 * core}, device_id_type=MESH,
        )
        copy.start()
        d_copies.append(copy)

    def place(hf, dp, dq):
        dx, dz = (dq, dp) if hf == 0 else (dp, dq)
        return 4 * lax.rem(x + dx % 4, 4) + lax.rem(z + dz % 4, 4)

    b_copies = []

    def send(hf, dp, dq, rh, ep, eq):
        copy = pltpu.make_async_remote_copy(
            src_ref=qg.at[hf, place(hf, dp, dq), rh], dst_ref=qg.at[hf, place(hf, dp, dq), rh],
            send_sem=b_send.at[len(b_copies)],
            recv_sem=b_recv.at[hf, (dq - eq) % 4, (dp - ep) % 4, rh],
            device_id={"sub": place(hf, ep, eq)}, device_id_type=MESH,
        )
        copy.start()
        b_copies.append(copy)

    def arrived(hf, dp, dq, rh):
        pltpu.make_async_remote_copy(
            src_ref=qg.at[hf, place(hf, dp, dq), rh], dst_ref=qg.at[hf, place(hf, dp, dq), rh],
            send_sem=b_send.at[0], recv_sem=b_recv.at[hf, dq % 4, dp % 4, rh],
            device_id={"sub": j}, device_id_type=MESH,
        ).wait_recv()

    four = ((0, 1), (0, -1), (1, 0), (-1, 0))
    for hf in range(2):
        for ep, eq in four:
            send(hf, 0, 0, core, ep, eq)
    for hf in range(2):
        pltpu.make_async_remote_copy(
            src_ref=ptn.at[hf], dst_ref=qg.at[hf, j, 1 - core],
            send_sem=d_send.at[hf], recv_sem=d_recv.at[hf],
            device_id={"facet": f + 1 - 2 * core}, device_id_type=MESH,
        ).wait_recv()
        for ep, eq in four:
            send(hf, 0, 0, 1 - core, ep, eq)

    for copy in m_copies:
        copy.wait_recv()
    step = meta_all[target[0, 0]][0:1, :] + 2044
    rows128 = iota((16, 128), 0)
    base_c, base_s = turn(((step * rows128) & (NIMG - 1)).astype(F32) * (1.0 / NIMG))
    for part in range(4):
        coarse_c, coarse_s = turn(((step * (16 * (iota((16, 128), 0) + 16 * part))) & (NIMG - 1)).astype(F32) * (1.0 / NIMG))
        for q in range(16):
            cc, cs = coarse_c[q : q + 1], coarse_s[q : q + 1]
            at = part * 256 + q * 16
            ec[at : at + 16] = base_c * cc - base_s * cs
            es[at : at + 16] = -(base_s * cc + base_c * cs)

    for dp in (-1, 1):
        for rh in range(2):
            for hf in range(2):
                arrived(hf, dp, 0, rh)
                send(hf, dp, 0, rh, 0, 1)
                send(hf, dp, 0, rh, 0, -1)
                if rh == (0 if dp == -1 else 1):
                    send(hf, dp, 0, rh, -dp, 0)

    rank = jnp.zeros((1, 128), F32)
    slots = [jnp.zeros((2, ROWS), F32) for _ in range(2)]
    for b in range(NS):
        match = jnp.where(meta_all[b, 1:2, :] == j, 1.0, 0.0)
        for slot in range(2):
            picked = jnp.where(rank == float(slot), match, 0.0)
            mask[slot, b : b + 1, :] = picked
            slots[slot] = slots[slot] + picked[:, 0:1] * pos_all[b]
        rank = rank + match
    for slot in range(2):
        slot_pos[slot] = slots[slot]

    def slot_table(slot, k):
        half_steps(slot_pos[slot, k : k + 1, :], ROWS, small)
        if k == 0:
            table_into(ubo, (slot,), BF16)
        else:
            table_into(vbo, (slot,), F32)

    def across(dp):
        for dq in (-1, 1):
            for rh in range(2):
                for hf in range(2):
                    arrived(hf, dp, dq, rh)
                    if rh == (0 if dq == -1 else 1):
                        send(hf, dp, dq, rh, 0, -dq)

    def transform(dq):
        for hf in range(2):
            line = lax.rem((x if hf == 0 else z) + dq % 4, 4)

            def modulate(i, carry, hf=hf, line=line):
                k4, rh = i // 2, lax.rem(i, 2)
                src = 4 * line + k4 if hf == 0 else 4 * k4 + line
                at = pl.multiple_of(src * 64 + rh * 32, 32)
                to = pl.multiple_of(i * 32, 32)
                c, s = ec[pl.ds(at, 32)], es[pl.ds(at, 32)]
                for k in range(2):
                    re = qg[hf, src, rh, :, k * 128 : k * 128 + 128].astype(F32)
                    im = qg[hf, src, rh, :, 256 + k * 128 : 384 + k * 128].astype(F32)
                    qm[hf, pl.ds(to, 32), k * 128 : k * 128 + 128] = (re * c - im * s).astype(BF16)
                    qm[hf, pl.ds(to, 32), 256 + k * 128 : 384 + k * 128] = (re * s + im * c).astype(BF16)
                return carry

            lax.fori_loop(0, 8, modulate, 0)
        for hf in range(2):
            line = lax.rem((x if hf == 0 else z) + dq % 4, 4)
            part = jnp.dot(
                bt[hf, :, pl.ds(pl.multiple_of(line * 256, 256), 256)], qm[hf], preferred_element_type=F32
            )
            if dq == 0:
                hacc[hf] = part
            elif dq == 2:
                both = (hacc[hf] + part).astype(BF16)
                hs[0:M, hf * HALF : hf * HALF + HALF] = both[:, 0:HALF]
                hs[M : 2 * M, hf * HALF : hf * HALF + HALF] = both[:, HALF:M]
            else:
                hacc[hf] += part

    across(0)
    slot_table(0, 0)
    for rh in range(2):
        for hf in range(2):
            arrived(hf, 2, 0, rh)
            send(hf, 2, 0, rh, 0, 1)
            send(hf, 2, 0, rh, 0, -1)
    slot_table(0, 1)
    across(-1)
    across(1)
    transform(0)
    slot_table(1, 0)
    across(2)
    slot_table(1, 1)
    transform(-1)
    transform(1)
    for dp in (0, -1, 1, 2):
        for rh in range(2):
            for hf in range(2):
                arrived(hf, dp, 2, rh)
    transform(2)

    live_count = count[0]

    for at in range(0, ROWS, 256):
        lifted = jnp.dot(hs[...], ub[:, pl.ds(at, 256)], preferred_element_type=F32)
        v = vb[:, pl.ds(at, 256)]
        sum_re = jnp.sum(lifted[0:M] * v, axis=0, keepdims=True)
        sum_im = jnp.sum(lifted[M : 2 * M] * v, axis=0, keepdims=True)
        c, s = turn((pos[0, 0:1, pl.ds(at, 256)] + pos[0, 1:2, pl.ds(at, 256)]) * 0.5)
        scale = 4.0 / (M * FS)
        live = iota((1, 256), 1) + at < live_count
        re = obs[0, 0:1, pl.ds(at, 256)] - (sum_re * c + sum_im * s) * scale
        im = obs[0, 1:2, pl.ds(at, 256)] - (sum_im * c - sum_re * s) * scale
        res_out[0, 0:1, pl.ds(at, 256)] = jnp.where(live, re, 0.0)
        res_out[0, 1:2, pl.ds(at, 256)] = jnp.where(live, im, 0.0)

    c_copies = []
    for d in range(1, NS):
        copy = pltpu.make_async_remote_copy(
            src_ref=res_out.at[0], dst_ref=res_all.at[j], send_sem=c_send.at[d - 1], recv_sem=c_recv.at[d - 1],
            device_id={"sub": lax.rem(j + d, NS)}, device_id_type=MESH,
        )
        copy.start()
        c_copies.append(copy)
    res_all[j] = res_out[0]
    for copy in a_copies + m_copies + d_copies + b_copies:
        copy.wait_send()
    for copy in c_copies:
        copy.wait()

    rows = []
    for slot in range(2):
        r = jnp.zeros((2, ROWS), F32)
        for b in range(NS):
            r = r + mask[slot, b : b + 1, 0:1] * res_all[b]
        p = slot_pos[slot]
        c, s = turn((p[0:1, :] + p[1:2, :]) * 0.5)
        rows.append((r[0:1, :] * c - r[1:2, :] * s, r[0:1, :] * s + r[1:2, :] * c))
    for block in range(4):
        im, sine = block // 2, block % 2
        for slot in range(2):
            wb[block, :, slot * ROWS : slot * ROWS + ROWS] = (
                vbo[slot, sine * HALF : sine * HALF + HALF, :] * rows[slot][im]
            ).astype(BF16)
        for k in range(2):
            total[k, block] = sum(
                lax.dot_general(
                    ubo[slot, k * HALF : k * HALF + HALF, :], wb[block, :, slot * ROWS : slot * ROWS + ROWS],
                    (((1,), (1,)), ((), ())), preferred_element_type=F32,
                )
                for slot in range(2)
            )

    scale = 1.0 / math.sqrt(ROWS)
    flip = jnp.where(iota((HALF, HALF), 0) + iota((HALF, HALF), 1) == HALF - 1, 1.0, 0.0).astype(BF16)

    def flip_columns(a):
        return jnp.dot(a.astype(BF16), flip, preferred_element_type=F32).astype(BF16)

    def flip_rows(a):
        return jnp.dot(flip, a, preferred_element_type=F32).astype(BF16)

    for im in range(2):
        sign = 1.0 if im == 0 else -1.0
        cc, ss = total[0, 2 * im], total[1, 2 * im + 1]
        cs, sc = total[0, 3 - 2 * im], total[1, 2 - 2 * im]
        even, both = (cc - ss) * scale, (cc + ss) * scale
        y, w = (cs + sc) * (scale * sign), (cs - sc) * (scale * sign)
        left, right = slice(im * M, im * M + HALF), slice(im * M + HALF, im * M + M)
        grid_out[0, 0, HALF:M, right] = (even + y).astype(BF16)
        grid_out[0, 0, HALF:M, left] = flip_columns(both - w)
        grid_out[0, 0, 0:HALF, right] = flip_rows((both + w).astype(BF16))
        grid_out[0, 0, 0:HALF, left] = flip_rows(flip_columns(even - y))


def per_device(facets, tapers, row_offsets, col_offsets, block_subgrid, vis_count, positions, observed):
    vmem = pl.BlockSpec(memory_space=pltpu.VMEM)
    smem = pl.BlockSpec(memory_space=pltpu.SMEM)
    dma = pltpu.SemaphoreType.DMA
    residual, grid = pl.pallas_call(
        front,
        out_shape=(
            jax.ShapeDtypeStruct((1, 2, ROWS), F32),
            jax.ShapeDtypeStruct((1, 1, M, 2 * M), BF16),
        ),
        in_specs=[pl.BlockSpec(memory_space=pl.ANY), vmem, smem, smem, smem, smem, vmem, vmem],
        out_specs=(vmem, vmem),
        scratch_shapes=[
            pltpu.VMEM((NS, 2, ROWS), F32),
            pltpu.VMEM((NS, 2, ROWS), F32),
            pltpu.VMEM((NS, 8, 128), I32),
            pltpu.VMEM((FS, 128), BF16),
            pltpu.VMEM((4, 32, FS), BF16),
            pltpu.VMEM((NF, 32, FS), BF16),
            pltpu.VMEM((2, M, FS), BF16),
            pltpu.VMEM((128, FS), BF16),
            pltpu.VMEM((2, 32, M), BF16),
            pltpu.VMEM((2, NS, 2, 32, M), BF16),
            pltpu.VMEM((2, 256, M), BF16),
            pltpu.VMEM((FS, 128), F32),
            pltpu.VMEM((FS, 128), F32),
            pltpu.VMEM((M, ROWS), BF16),
            pltpu.VMEM((M, ROWS), F32),
            pltpu.VMEM((2 * M, M), BF16),
            pltpu.VMEM((2, M, M), F32),
            pltpu.VMEM((4, 16, FS), F32),
            pltpu.VMEM((8, 128), I32),
            pltpu.VMEM((2, NS, 128), F32),
            pltpu.VMEM((2, 2, ROWS), F32),
            pltpu.VMEM((2, M, ROWS), BF16),
            pltpu.VMEM((2, M, ROWS), F32),
            pltpu.VMEM((4, HALF, 2 * ROWS), BF16),
            pltpu.VMEM((2, 4, HALF, HALF), F32),
            dma(()),
            dma((NF - 1,)), dma((NF - 1,)),
            dma((2,)), dma((2,)),
            dma((60,)), dma((2, 4, 4, 2)),
            dma((NS - 1,)), dma((NS - 1,)),
            dma((NS - 1,)), dma((NS - 1,)),
            dma((NS - 1,)), dma((NS - 1,)),
        ],
        compiler_params=pltpu.CompilerParams(collective_id=0, has_side_effects=True),
        name="front",
    )(facets, tapers, row_offsets, col_offsets, block_subgrid, vis_count, positions, observed)
    return residual, grid.astype(F32)


def solution(mesh):
    in_specs = (
        P("facet", None, None),
        P(),
        P(),
        P("sub"),
        P(("facet", "sub"), None),
        P(("facet", "sub")),
        P(("facet", "sub"), None, None),
        P(("facet", "sub"), None, None),
    )
    out_specs = (P(("facet", "sub"), None, None), P("facet", "sub", None, None))
    return jax.shard_map(per_device, mesh=mesh, in_specs=in_specs, out_specs=out_specs, check_vma=False)
```

```python
import functools
import math

import jax
import jax.numpy as jnp
from jax import lax
from jax.experimental import pallas as pl
from jax.experimental.pallas import tpu as pltpu
from jax.sharding import PartitionSpec as P

M = 512
HALF = 256
FS = 1024
NIMG = 8192
ROWS = 1024
NF = 8
NS = 16
MESH = pl.DeviceIdType.MESH
F32 = jnp.float32
BF16 = jnp.bfloat16
I32 = jnp.int32


def turn(t):
    u = (t - jnp.round(t)) * math.pi
    v = u * u
    s = 1.0 / 6227020800.0
    for c in (-1.0 / 39916800.0, 1.0 / 362880.0, -1.0 / 5040.0, 1.0 / 120.0, -1.0 / 6.0, 1.0):
        s = s * v + c
    s = s * u
    k = 1.0 / 479001600.0
    for c in (-1.0 / 3628800.0, 1.0 / 40320.0, -1.0 / 720.0, 1.0 / 24.0, -0.5, 1.0):
        k = k * v + c
    return 1.0 - 2.0 * s * s, 2.0 * s * k


def grow(base, coarse, steps, put):
    bc, bs = base

    def step(q, carry):
        cc, cs = coarse(q)
        put(q, bc * cc - bs * cs, bs * cc + bc * cs)
        return carry

    lax.fori_loop(0, steps, step, 0)


def iota(shape, dim):
    return lax.broadcasted_iota(I32, shape, dim)


def half_steps(p, n, m_ref, start=0.0):
    shape = (16, n)
    rows = iota(shape, 0).astype(F32)
    m_ref[0], m_ref[1] = turn(p * (rows + 0.5))
    m_ref[2], m_ref[3] = turn(p * (rows * 16.0 + start))


def basis_into(m_ref, lanes, put, steps=16):
    for at, width in lanes:
        base = (m_ref[0, :, pl.ds(at, width)], m_ref[1, :, pl.ds(at, width)])

        def coarse(q, at=at, width=width):
            return m_ref[2, pl.ds(q, 1), pl.ds(at, width)], m_ref[3, pl.ds(q, 1), pl.ds(at, width)]

        def put_here(q, c, s, at=at, width=width):
            put(pl.multiple_of(q * 16, 16), at, width, c, s)

        grow(base, coarse, steps, put_here)


def front(
    facets, taper_in, row_off_in, col_off_in, target_in, count_in, pos_in, obs_in,
    res_out, grid_out,
    tapers, pos, obs, row_off, col_off, target, count, res_src,
    res_all, pos_all, meta_all, fac, tt, facs, bt, zs, uq, qg, qm, ec, es, ub, vb, hs, hacc, small, meta_src,
    mask, slot_pos, ubo, vbo, wb, total, part_out, part_in,
    load_sem, a_send, a_recv, d_send, d_recv, b_send, b_recv, m_send, m_recv, p_send, p_recv, c_send, c_recv,
):
    f = lax.axis_index("facet")
    j = lax.axis_index("sub")
    core = lax.rem(f, 2)
    x, z = j // 4, lax.rem(j, 4)
    pair, odd = j // 2, lax.rem(j, 2)
    at128 = pl.multiple_of(pair * 128, 128)

    y = f // 2
    barrier = pltpu.get_barrier_semaphore()
    near = [2 * lax.rem(y + dy, 4) + c for dy in (1, 3) for c in range(2)] + [f + 1 - 2 * core]
    for peer in near:
        pl.semaphore_signal(barrier, inc=1, device_id={"facet": peer}, device_id_type=MESH)
    for d in range(1, NS):
        pl.semaphore_signal(barrier, inc=1, device_id={"sub": lax.rem(j + d, NS)}, device_id_type=MESH)
    for dz in range(1, 4):
        other = {"facet": f + 1 - 2 * core, "sub": 4 * x + lax.rem(z + dz, 4)}
        pl.semaphore_signal(barrier, inc=1, device_id=other, device_id_type=MESH)
    loads = [
        pltpu.make_async_copy(src, dst, load_sem.at[i])
        for i, (src, dst) in enumerate((
            (facets.at[0, :, pl.ds(at128, 128)], fac), (taper_in, tapers), (pos_in, pos), (obs_in, obs),
            (row_off_in, row_off), (col_off_in, col_off), (target_in, target), (count_in, count),
        ))
    ]
    for load in loads:
        load.start()
    for load in loads:
        load.wait()

    rows8 = iota((8, 128), 0)
    meta_src[...] = jnp.where(rows8 == 0, col_off[0], jnp.where(rows8 == 1, target[0, 0], count[0]))
    meta_all[j] = meta_src[...]
    pos_all[j] = pos[0]

    by_column = fac[...].astype(F32) * tapers[1:2, pl.ds(at128, 128)]
    turned = (by_column.T * tapers[0:1, :]).astype(BF16)
    for g in range(4):
        tt[g] = turned[g * 32 : g * 32 + 32]
    facs[f] = tt[2 * odd + core]

    pl.semaphore_wait(barrier, 5 + NS - 1 + 3)
    a_copies, m_copies = [], []

    def facet_at(dy, c):
        return 2 * lax.rem(y + dy % 4, 4) + c

    def send_slice(src, source, dy, c, slot):
        copy = pltpu.make_async_remote_copy(
            src_ref=src, dst_ref=facs.at[source], send_sem=a_send.at[len(a_copies)], recv_sem=a_recv.at[slot],
            device_id={"facet": facet_at(dy, c)}, device_id_type=MESH,
        )
        copy.start()
        a_copies.append(copy)

    def slice_arrived(dy, c, slot):
        pltpu.make_async_remote_copy(
            src_ref=facs.at[facet_at(dy, c)], dst_ref=facs.at[facet_at(dy, c)],
            send_sem=a_send.at[0], recv_sem=a_recv.at[slot], device_id={"facet": f}, device_id_type=MESH,
        ).wait_recv()

    for dy in (1, 3):
        for c in range(2):
            send_slice(tt.at[2 * odd + c], f, dy, c, 2 * (4 - dy) + core)
    send_slice(tt.at[2 * odd + 1 - core], f, 0, 1 - core, 0)
    for d in range(1, NS):
        peer = lax.rem(j + d, NS)
        for src, dst, ss, rs in ((meta_src, meta_all, m_send, m_recv), (pos.at[0], pos_all, p_send, p_recv)):
            copy = pltpu.make_async_remote_copy(
                src_ref=src, dst_ref=dst.at[j], send_sem=ss.at[d - 1], recv_sem=rs.at[d - 1],
                device_id={"sub": peer}, device_id_type=MESH,
            )
            copy.start()
            m_copies.append(copy)

    lanes4 = [(0, 256), (256, 256), (512, 256), (768, 256)]

    def table_into(ref, lead, dtype):
        def put(at, lane_at, width, c, s):
            ref[(*lead, pl.ds(at, 16), pl.ds(lane_at, width))] = c.astype(dtype)
            ref[(*lead, pl.ds(at + HALF, 16), pl.ds(lane_at, width))] = s.astype(dtype)

        basis_into(small, lanes4, put)

    def relay_slices():
        slice_arrived(3, 0, 6)
        send_slice(facs.at[facet_at(3, 0)], facet_at(3, 0), 1, core, 4)
        slice_arrived(1, 1, 3)
        send_slice(facs.at[facet_at(1, 1)], facet_at(1, 1), 3, core, 5)

    lane = iota((16, FS), 1)
    row = iota((16, FS), 0)
    small[0], small[1] = turn((((2 * row + 1) * lane) & 2047).astype(F32) * (1.0 / 2048))
    small[2], small[3] = turn(((32 * row * lane) & 2047).astype(F32) * (1.0 / 2048))
    table_into(bt, (), BF16)
    relay_slices()

    phases = []
    rows_f = iota((NF, FS), 0)
    lane_f = iota((NF, FS), 1)
    for aa in range(2):
        off = row_off[2 * (f // 2) + aa]
        r = (off * (rows_f * FS + lane_f) + 2044 * lane_f) & (NIMG - 1)
        c, s = turn(r.astype(F32) * (1.0 / NIMG))
        phases.append((c, -s))

    slice_arrived(0, 1 - core, 0)
    slice_arrived(3, 1, 7)
    slice_arrived(1, 0, 2)
    slice_arrived(2, 0, 4)
    slice_arrived(2, 1, 5)
    for at, width in lanes4:
        sums = [jnp.zeros((32, width), F32) for _ in range(4)]
        for g in range(NF):
            t = facs[g, :, at : at + width].astype(F32)
            for aa in range(2):
                sums[2 * aa] = sums[2 * aa] + t * phases[aa][0][g : g + 1, at : at + width]
                sums[2 * aa + 1] = sums[2 * aa + 1] + t * phases[aa][1][g : g + 1, at : at + width]
        for i in range(4):
            zs[i * 32 : i * 32 + 32, at : at + width] = sums[i].astype(BF16)
    turned_rows = lax.dot_general(
        zs[...], bt[...], (((1,), (1,)), ((), ())), preferred_element_type=F32
    ).astype(BF16)
    for aa in range(2):
        for k in range(4):
            uq[aa, k] = jnp.concatenate([
                turned_rows[aa * 64 : aa * 64 + 32, k * 128 : k * 128 + 128],
                turned_rows[aa * 64 + 32 : aa * 64 + 64, k * 128 : k * 128 + 128],
            ], axis=1)
    qg[j, core] = uq[core, z]

    def place(dx, dz):
        return 4 * lax.rem(x + dx % 4, 4) + lax.rem(z + dz % 4, 4)

    def core_of(e):
        return core if e == 0 else 1 - core

    b_copies = []

    def send_unit(src, dst, slot, device):
        copy = pltpu.make_async_remote_copy(
            src_ref=src, dst_ref=dst, send_sem=b_send.at[len(b_copies)], recv_sem=b_recv.at[slot],
            device_id=device, device_id_type=MESH,
        )
        copy.start()
        b_copies.append(copy)

    def slot_of(dx, dz, e):
        return ((dx % 4) * 4 + dz % 4) * 2 + e

    def unit(dx, dz, e):
        return qg.at[place(dx, dz), core_of(e)]

    def along_x(dx, dz, e, ex):
        send_unit(unit(dx, dz, e), unit(dx, dz, e), slot_of(dx - ex, dz, e), {"sub": place(ex, 0)})

    def arrived(dx, dz, e):
        pltpu.make_async_remote_copy(
            src_ref=unit(dx, dz, e), dst_ref=unit(dx, dz, e), send_sem=b_send.at[0],
            recv_sem=b_recv.at[slot_of(dx, dz, e)], device_id={"sub": j}, device_id_type=MESH,
        ).wait_recv()

    for dz in (2, 1, -1, 0):
        for e in range(2):
            if dz or e:
                send_unit(
                    uq.at[core_of(e), lax.rem(z + dz % 4, 4)], qg.at[j, core], slot_of(0, -dz, e),
                    {"facet": 2 * y + core_of(e), "sub": place(0, dz)},
                )
    along_x(0, 0, 0, 1)
    along_x(0, 0, 0, -1)

    for copy in m_copies:
        copy.wait_recv()

    def column_phase(k):
        offset = jnp.zeros((1, 128), I32)
        for b in range(NS):
            offset = offset + jnp.where(meta_all[4 * x + k, 1:2, :] == b, meta_all[b, 0:1, :], 0)
        step = offset + 2044
        rows128 = iota((16, 128), 0)
        base_c, base_s = turn(((step * rows128) & (NIMG - 1)).astype(F32) * (1.0 / NIMG))
        for part in range(4):
            coarse_c, coarse_s = turn(((step * (16 * (rows128 + 16 * part))) & (NIMG - 1)).astype(F32) * (1.0 / NIMG))
            for q in range(16):
                cc, cs = coarse_c[q : q + 1], coarse_s[q : q + 1]
                at = part * 256 + q * 16
                ec[k, at : at + 16] = base_c * cc - base_s * cs
                es[k, at : at + 16] = -(base_s * cc + base_c * cs)

    def column_basis(k):
        half_steps(pos_all[4 * x + k, 1:2, :], ROWS, small)
        table_into(vb, (k,), BF16)

    def row_quarter(k):
        half_steps(pos_all[4 * x + k, 0:1, :], ROWS, small, 128.0 * lax.rem(z, 2).astype(F32))

        def put(at, lane_at, width, c, s):
            ub[k, pl.ds(at, 16), pl.ds(lane_at, width)] = jnp.where(z < 2, c, s)

        basis_into(small, lanes4, put, 8)

    def from_line(dz, e):
        arrived(0, dz, e)
        along_x(0, dz, e, 1)
        along_x(0, dz, e, -1)

    def across(dz):
        for e in range(2):
            for dx in (-1, 1):
                arrived(dx, dz, e)
                if e == (0 if dx == -1 else 1):
                    along_x(dx, dz, e, -dx)

    def transform(dx):
        line = lax.rem(x + dx % 4, 4)

        def modulate(i, carry):
            zz, cc = i // 2, lax.rem(i, 2)
            src = 4 * line + zz
            at = pl.multiple_of(src * 64 + cc * 32, 32)
            to = pl.multiple_of(i * 32, 32)
            re = qg[src, cc, :, 0:128].astype(F32)
            im = qg[src, cc, :, 128:256].astype(F32)
            for k in range(4):
                c, s = ec[k, pl.ds(at, 32)], es[k, pl.ds(at, 32)]
                qm[pl.ds(to, 32), k * 256 : k * 256 + 128] = (re * c - im * s).astype(BF16)
                qm[pl.ds(to, 32), k * 256 + 128 : k * 256 + 256] = (re * s + im * c).astype(BF16)
            return carry

        lax.fori_loop(0, 8, modulate, 0)
        lanes = pl.ds(pl.multiple_of(line * 256, 256), 256)
        for k in range(4):
            part = jnp.dot(bt[:, lanes], qm[:, k * 256 : k * 256 + 256], preferred_element_type=F32)
            if dx == 0:
                hacc[k] = part
            elif dx == 2:
                hs[k] = (hacc[k] + part).T.astype(BF16)
            else:
                hacc[k] += part

    column_phase(0)
    from_line(0, 1)
    column_phase(1)
    for dz in (-1, 1):
        for e in range(2):
            from_line(dz, e)
    column_phase(2)
    for e in range(2):
        from_line(2, e)
    column_phase(3)
    across(0)
    transform(0)
    column_basis(0)
    across(-1)
    column_basis(1)
    across(1)
    column_basis(2)
    across(2)
    column_basis(3)
    transform(-1)
    transform(1)
    for k in range(4):
        row_quarter(k)
    for dz in (0, -1, 1, 2):
        for e in range(2):
            arrived(2, dz, e)
    transform(2)

    part_copies = []
    for dz in (2, 1, -1, 0):
        k = lax.rem(z + dz % 4, 4)
        for at in range(0, ROWS, 256):
            lifted = jnp.dot(hs[k], vb[k, :, at : at + 256], preferred_element_type=F32)
            u = ub[k, :, at : at + 256]
            part_out[dz % 4, 0:1, at : at + 256] = jnp.sum(lifted[0:128] * u, axis=0, keepdims=True)
            part_out[dz % 4, 1:2, at : at + 256] = jnp.sum(lifted[128:256] * u, axis=0, keepdims=True)
        if dz:
            copy = pltpu.make_async_remote_copy(
                src_ref=part_out.at[dz % 4], dst_ref=part_in.at[-dz % 4],
                send_sem=d_send.at[dz % 4], recv_sem=d_recv.at[-dz % 4],
                device_id={"sub": place(0, dz)}, device_id_type=MESH,
            )
            copy.start()
            part_copies.append(copy)
    for copy in part_copies:
        copy.wait_recv()

    live_count = count[0]

    sums = part_out[0] + part_in[1] + part_in[2] + part_in[3]
    sum_re, sum_im = sums[0:1], sums[1:2]
    c, s = turn((pos[0, 0:1, :] + pos[0, 1:2, :]) * 0.5)
    scale = 4.0 / (M * FS)
    live = iota((1, ROWS), 1) < live_count
    re = obs[0, 0:1, :] - (sum_re * c + sum_im * s) * scale
    im = obs[0, 1:2, :] - (sum_im * c - sum_re * s) * scale
    both = jnp.concatenate([jnp.where(live, re, 0.0), jnp.where(live, im, 0.0)], axis=0)
    res_out[0] = both
    res_src[...] = both.astype(BF16)

    c_copies = []
    for d in range(1, NS):
        copy = pltpu.make_async_remote_copy(
            src_ref=res_src, dst_ref=res_all.at[j], send_sem=c_send.at[d - 1], recv_sem=c_recv.at[d - 1],
            device_id={"sub": lax.rem(j + d, NS)}, device_id_type=MESH,
        )
        copy.start()
        c_copies.append(copy)
    res_all[j] = res_src[...]

    rank = jnp.zeros((1, 128), F32)
    slots = [jnp.zeros((2, ROWS), F32) for _ in range(2)]
    for b in range(NS):
        match = jnp.where(meta_all[b, 1:2, :] == j, 1.0, 0.0)
        for slot in range(2):
            picked = jnp.where(rank == float(slot), match, 0.0)
            mask[slot, b : b + 1, :] = picked
            slots[slot] = slots[slot] + picked[:, 0:1] * pos_all[b]
        rank = rank + match
    for slot in range(2):
        slot_pos[slot] = slots[slot]
    for slot in range(2):
        half_steps(slot_pos[slot, 0:1, :], ROWS, small)
        table_into(ubo, (slot,), BF16)
        half_steps(slot_pos[slot, 1:2, :], ROWS, small)
        table_into(vbo, (slot,), F32)

    for copy in a_copies + m_copies + b_copies + part_copies:
        copy.wait_send()
    for copy in c_copies:
        copy.wait()

    rows = []
    for slot in range(2):
        r = jnp.zeros((2, ROWS), F32)
        for b in range(NS):
            r = r + mask[slot, b : b + 1, 0:1] * res_all[b].astype(F32)
        p = slot_pos[slot]
        c, s = turn((p[0:1, :] + p[1:2, :]) * 0.5)
        rows.append((r[0:1, :] * c - r[1:2, :] * s, r[0:1, :] * s + r[1:2, :] * c))
    for block in range(4):
        im, sine = block // 2, block % 2
        for slot in range(2):
            wb[block, :, slot * ROWS : slot * ROWS + ROWS] = (
                vbo[slot, sine * HALF : sine * HALF + HALF, :] * rows[slot][im]
            ).astype(BF16)
        for k in range(2):
            total[k, block] = sum(
                lax.dot_general(
                    ubo[slot, k * HALF : k * HALF + HALF, :], wb[block, :, slot * ROWS : slot * ROWS + ROWS],
                    (((1,), (1,)), ((), ())), preferred_element_type=F32,
                )
                for slot in range(2)
            )

    scale = 1.0 / math.sqrt(ROWS)
    flip = jnp.where(iota((HALF, HALF), 0) + iota((HALF, HALF), 1) == HALF - 1, 1.0, 0.0).astype(BF16)

    def flip_columns(a):
        return jnp.dot(a.astype(BF16), flip, preferred_element_type=F32).astype(BF16)

    def flip_rows(a):
        return jnp.dot(flip, a, preferred_element_type=F32).astype(BF16)

    for im in range(2):
        sign = 1.0 if im == 0 else -1.0
        cc, ss = total[0, 2 * im], total[1, 2 * im + 1]
        cs, sc = total[0, 3 - 2 * im], total[1, 2 - 2 * im]
        even, both = (cc - ss) * scale, (cc + ss) * scale
        y, w = (cs + sc) * (scale * sign), (cs - sc) * (scale * sign)
        left, right = slice(im * M, im * M + HALF), slice(im * M + HALF, im * M + M)
        grid_out[0, 0, HALF:M, right] = (even + y).astype(BF16)
        grid_out[0, 0, HALF:M, left] = flip_columns(both - w)
        grid_out[0, 0, 0:HALF, right] = flip_rows((both + w).astype(BF16))
        grid_out[0, 0, 0:HALF, left] = flip_rows(flip_columns(even - y))


def widen(res_in, grid_in, res_out, grid_out):
    res_out[...] = res_in[...]
    grid_out[...] = grid_in[...].astype(F32)


def per_device(facets, tapers, row_offsets, col_offsets, block_subgrid, vis_count, positions, observed):
    vmem = pl.BlockSpec(memory_space=pltpu.VMEM)
    dma = pltpu.SemaphoreType.DMA
    residual, grid = pl.pallas_call(
        front,
        out_shape=(
            jax.ShapeDtypeStruct((1, 2, ROWS), F32),
            jax.ShapeDtypeStruct((1, 1, M, 2 * M), BF16),
        ),
        in_specs=[pl.BlockSpec(memory_space=pltpu.HBM)] * 8,
        out_specs=(vmem, vmem),
        scratch_shapes=[
            pltpu.VMEM((2, FS), F32),
            pltpu.VMEM((1, 2, ROWS), F32),
            pltpu.VMEM((1, 2, ROWS), F32),
            pltpu.SMEM((NF,), I32),
            pltpu.SMEM((1,), I32),
            pltpu.SMEM((1, 1), I32),
            pltpu.SMEM((1,), I32),
            pltpu.VMEM((2, ROWS), BF16),
            pltpu.VMEM((NS, 2, ROWS), BF16),
            pltpu.VMEM((NS, 2, ROWS), F32),
            pltpu.VMEM((NS, 8, 128), I32),
            pltpu.VMEM((FS, 128), BF16),
            pltpu.VMEM((4, 32, FS), BF16),
            pltpu.VMEM((NF, 32, FS), BF16),
            pltpu.VMEM((M, FS), BF16),
            pltpu.VMEM((128, FS), BF16),
            pltpu.VMEM((2, 4, 32, 256), BF16),
            pltpu.VMEM((NS, 2, 32, 256), BF16),
            pltpu.VMEM((256, 1024), BF16),
            pltpu.VMEM((4, FS, 128), F32),
            pltpu.VMEM((4, FS, 128), F32),
            pltpu.VMEM((4, 128, ROWS), F32),
            pltpu.VMEM((4, M, ROWS), BF16),
            pltpu.VMEM((4, 256, M), BF16),
            pltpu.VMEM((4, M, 256), F32),
            pltpu.VMEM((4, 16, FS), F32),
            pltpu.VMEM((8, 128), I32),
            pltpu.VMEM((2, NS, 128), F32),
            pltpu.VMEM((2, 2, ROWS), F32),
            pltpu.VMEM((2, M, ROWS), BF16),
            pltpu.VMEM((2, M, ROWS), F32),
            pltpu.VMEM((4, HALF, 2 * ROWS), BF16),
            pltpu.VMEM((2, 4, HALF, HALF), F32),
            pltpu.VMEM((4, 2, ROWS), F32),
            pltpu.VMEM((4, 2, ROWS), F32),
            dma((8,)),
            dma((NF - 1,)), dma((8,)),
            dma((4,)), dma((4,)),
            dma((32,)), dma((32,)),
            dma((NS - 1,)), dma((NS - 1,)),
            dma((NS - 1,)), dma((NS - 1,)),
            dma((NS - 1,)), dma((NS - 1,)),
        ],
        compiler_params=pltpu.CompilerParams(collective_id=0, has_side_effects=True),
        name="front",
    )(facets, tapers, row_offsets, col_offsets, block_subgrid, vis_count, positions, observed)
    return pl.pallas_call(
        widen,
        out_shape=(
            jax.ShapeDtypeStruct((1, 2, ROWS), F32),
            jax.ShapeDtypeStruct((1, 1, M, 2 * M), F32),
        ),
        in_specs=[vmem, vmem],
        out_specs=(vmem, vmem),
        name="widen",
    )(residual, grid)


def solution(mesh):
    in_specs = (
        P("facet", None, None),
        P(),
        P(),
        P("sub"),
        P(("facet", "sub"), None),
        P(("facet", "sub")),
        P(("facet", "sub"), None, None),
        P(("facet", "sub"), None, None),
    )
    out_specs = (P(("facet", "sub"), None, None), P("facet", "sub", None, None))
    return jax.shard_map(per_device, mesh=mesh, in_specs=in_specs, out_specs=out_specs, check_vma=False)
```

```python
import functools
import math

import jax
import jax.numpy as jnp
from jax import lax
from jax.experimental import pallas as pl
from jax.experimental.pallas import tpu as pltpu
from jax.sharding import PartitionSpec as P

M = 512
HALF = 256
FS = 1024
NIMG = 8192
ROWS = 1024
NF = 8
NS = 16
MESH = pl.DeviceIdType.MESH
F32 = jnp.float32
BF16 = jnp.bfloat16
I32 = jnp.int32


def turn(t):
    u = (t - jnp.round(t)) * math.pi
    v = u * u
    s = 1.0 / 6227020800.0
    for c in (-1.0 / 39916800.0, 1.0 / 362880.0, -1.0 / 5040.0, 1.0 / 120.0, -1.0 / 6.0, 1.0):
        s = s * v + c
    s = s * u
    k = 1.0 / 479001600.0
    for c in (-1.0 / 3628800.0, 1.0 / 40320.0, -1.0 / 720.0, 1.0 / 24.0, -0.5, 1.0):
        k = k * v + c
    return 1.0 - 2.0 * s * s, 2.0 * s * k


def grow(base, coarse, steps, put):
    bc, bs = base

    def step(q, carry):
        cc, cs = coarse(q)
        put(q, bc * cc - bs * cs, bs * cc + bc * cs)
        return carry

    lax.fori_loop(0, steps, step, 0)


def iota(shape, dim):
    return lax.broadcasted_iota(I32, shape, dim)


def half_steps(p, n, m_ref, start=0.0):
    shape = (16, n)
    rows = iota(shape, 0).astype(F32)
    m_ref[0], m_ref[1] = turn(p * (rows + 0.5))
    m_ref[2], m_ref[3] = turn(p * (rows * 16.0 + start))


def basis_into(m_ref, lanes, put, steps=16):
    for at, width in lanes:
        base = (m_ref[0, :, pl.ds(at, width)], m_ref[1, :, pl.ds(at, width)])

        def coarse(q, at=at, width=width):
            return m_ref[2, pl.ds(q, 1), pl.ds(at, width)], m_ref[3, pl.ds(q, 1), pl.ds(at, width)]

        def put_here(q, c, s, at=at, width=width):
            put(pl.multiple_of(q * 16, 16), at, width, c, s)

        grow(base, coarse, steps, put_here)


def front(
    facets, taper_in, row_off_in, col_off_in, target_in, count_in, pos_in, obs_in,
    res_out, grid_out,
    tapers, pos, obs, row_off, col_off, target, count, res_src,
    res_all, pos_all, meta_all, fac, tt, facs, bt, zs, uq, qg, qm, ec, es, ub, vb, hs, hacc, small, meta_src,
    mask, slot_pos, ubo, vbo, wb, total, part_out, part_in,
    load_sem, a_send, a_recv, d_send, d_recv, b_send, b_recv, m_send, m_recv, p_send, p_recv, c_send, c_recv,
):
    f = lax.axis_index("facet")
    j = lax.axis_index("sub")
    core = lax.rem(f, 2)
    x, z = j // 4, lax.rem(j, 4)
    pair, odd = j // 2, lax.rem(j, 2)
    at128 = pl.multiple_of(pair * 128, 128)

    y = f // 2
    barrier = pltpu.get_barrier_semaphore()
    near = [2 * lax.rem(y + dy, 4) + c for dy in (1, 3) for c in range(2)] + [f + 1 - 2 * core]
    for peer in near:
        pl.semaphore_signal(barrier, inc=1, device_id={"facet": peer}, device_id_type=MESH)
    for d in range(1, NS):
        pl.semaphore_signal(barrier, inc=1, device_id={"sub": lax.rem(j + d, NS)}, device_id_type=MESH)
    for dz in range(1, 4):
        other = {"facet": f + 1 - 2 * core, "sub": 4 * x + lax.rem(z + dz, 4)}
        pl.semaphore_signal(barrier, inc=1, device_id=other, device_id_type=MESH)
    loads = [
        pltpu.make_async_copy(src, dst, load_sem.at[i])
        for i, (src, dst) in enumerate((
            (facets.at[0, :, pl.ds(at128, 128)], fac), (taper_in, tapers), (pos_in, pos), (obs_in, obs),
            (row_off_in, row_off), (col_off_in, col_off), (target_in, target), (count_in, count),
        ))
    ]
    for load in loads:
        load.start()
    for load in loads:
        load.wait()

    rows8 = iota((8, 128), 0)
    meta_src[...] = jnp.where(rows8 == 0, col_off[0], jnp.where(rows8 == 1, target[0, 0], count[0]))
    meta_all[j] = meta_src[...]
    pos_all[j] = pos[0]

    by_column = fac[...].astype(F32) * tapers[1:2, pl.ds(at128, 128)]
    turned = (by_column.T * tapers[0:1, :]).astype(BF16)
    for g in range(4):
        tt[g] = turned[g * 32 : g * 32 + 32]
    facs[f] = tt[2 * odd + core]

    pl.semaphore_wait(barrier, 5 + NS - 1 + 3)
    a_copies, m_copies = [], []

    def facet_at(dy, c):
        return 2 * lax.rem(y + dy % 4, 4) + c

    def send_slice(src, source, dy, c, slot):
        copy = pltpu.make_async_remote_copy(
            src_ref=src, dst_ref=facs.at[source], send_sem=a_send.at[len(a_copies)], recv_sem=a_recv.at[slot],
            device_id={"facet": facet_at(dy, c)}, device_id_type=MESH,
        )
        copy.start()
        a_copies.append(copy)

    def slice_arrived(dy, c, slot):
        pltpu.make_async_remote_copy(
            src_ref=facs.at[facet_at(dy, c)], dst_ref=facs.at[facet_at(dy, c)],
            send_sem=a_send.at[0], recv_sem=a_recv.at[slot], device_id={"facet": f}, device_id_type=MESH,
        ).wait_recv()

    for dy in (1, 3):
        for c in range(2):
            send_slice(tt.at[2 * odd + c], f, dy, c, 2 * (4 - dy) + core)
    send_slice(tt.at[2 * odd + 1 - core], f, 0, 1 - core, 0)
    for d in range(1, NS):
        peer = lax.rem(j + d, NS)
        for src, dst, ss, rs in ((meta_src, meta_all, m_send, m_recv), (pos.at[0], pos_all, p_send, p_recv)):
            copy = pltpu.make_async_remote_copy(
                src_ref=src, dst_ref=dst.at[j], send_sem=ss.at[d - 1], recv_sem=rs.at[d - 1],
                device_id={"sub": peer}, device_id_type=MESH,
            )
            copy.start()
            m_copies.append(copy)

    lanes4 = [(0, 256), (256, 256), (512, 256), (768, 256)]

    def table_into(ref, lead, dtype):
        def put(at, lane_at, width, c, s):
            ref[(*lead, pl.ds(at, 16), pl.ds(lane_at, width))] = c.astype(dtype)
            ref[(*lead, pl.ds(at + HALF, 16), pl.ds(lane_at, width))] = s.astype(dtype)

        basis_into(small, lanes4, put)

    def relay_slices():
        slice_arrived(3, 0, 6)
        send_slice(facs.at[facet_at(3, 0)], facet_at(3, 0), 1, core, 4)
        slice_arrived(1, 1, 3)
        send_slice(facs.at[facet_at(1, 1)], facet_at(1, 1), 3, core, 5)

    lane = iota((16, FS), 1)
    row = iota((16, FS), 0)
    small[0], small[1] = turn((((2 * row + 1) * lane) & 2047).astype(F32) * (1.0 / 2048))
    small[2], small[3] = turn(((32 * row * lane) & 2047).astype(F32) * (1.0 / 2048))
    table_into(bt, (), BF16)
    relay_slices()

    phases = []
    rows_f = iota((NF, FS), 0)
    lane_f = iota((NF, FS), 1)
    for aa in range(2):
        off = row_off[2 * (f // 2) + aa]
        r = (off * (rows_f * FS + lane_f) + 2044 * lane_f) & (NIMG - 1)
        c, s = turn(r.astype(F32) * (1.0 / NIMG))
        phases.append((c, -s))

    slice_arrived(0, 1 - core, 0)
    slice_arrived(3, 1, 7)
    slice_arrived(1, 0, 2)
    slice_arrived(2, 0, 4)
    slice_arrived(2, 1, 5)
    for at, width in lanes4:
        sums = [jnp.zeros((32, width), F32) for _ in range(4)]
        for g in range(NF):
            t = facs[g, :, at : at + width].astype(F32)
            for aa in range(2):
                sums[2 * aa] = sums[2 * aa] + t * phases[aa][0][g : g + 1, at : at + width]
                sums[2 * aa + 1] = sums[2 * aa + 1] + t * phases[aa][1][g : g + 1, at : at + width]
        for i in range(4):
            zs[i * 32 : i * 32 + 32, at : at + width] = sums[i].astype(BF16)
    turned_rows = lax.dot_general(
        zs[...], bt[...], (((1,), (1,)), ((), ())), preferred_element_type=F32
    ).astype(BF16)
    for aa in range(2):
        for k in range(4):
            uq[aa, k] = jnp.concatenate([
                turned_rows[aa * 64 : aa * 64 + 32, k * 128 : k * 128 + 128],
                turned_rows[aa * 64 + 32 : aa * 64 + 64, k * 128 : k * 128 + 128],
            ], axis=1)
    qg[j, core] = uq[core, z]

    def place(dx, dz):
        return 4 * lax.rem(x + dx % 4, 4) + lax.rem(z + dz % 4, 4)

    def core_of(e):
        return core if e == 0 else 1 - core

    b_copies = []

    def send_unit(src, dst, slot, device):
        copy = pltpu.make_async_remote_copy(
            src_ref=src, dst_ref=dst, send_sem=b_send.at[len(b_copies)], recv_sem=b_recv.at[slot],
            device_id=device, device_id_type=MESH,
        )
        copy.start()
        b_copies.append(copy)

    def slot_of(dx, dz, e):
        return ((dx % 4) * 4 + dz % 4) * 2 + e

    def unit(dx, dz, e):
        return qg.at[place(dx, dz), core_of(e)]

    def along_x(dx, dz, e, ex):
        send_unit(unit(dx, dz, e), unit(dx, dz, e), slot_of(dx - ex, dz, e), {"sub": place(ex, 0)})

    def arrived(dx, dz, e):
        pltpu.make_async_remote_copy(
            src_ref=unit(dx, dz, e), dst_ref=unit(dx, dz, e), send_sem=b_send.at[0],
            recv_sem=b_recv.at[slot_of(dx, dz, e)], device_id={"sub": j}, device_id_type=MESH,
        ).wait_recv()

    for dz in (2, 1, -1, 0):
        for e in range(2):
            if dz or e:
                send_unit(
                    uq.at[core_of(e), lax.rem(z + dz % 4, 4)], qg.at[j, core], slot_of(0, -dz, e),
                    {"facet": 2 * y + core_of(e), "sub": place(0, dz)},
                )
    along_x(0, 0, 0, 1)
    along_x(0, 0, 0, -1)

    for copy in m_copies:
        copy.wait_recv()

    def column_phase(k):
        offset = jnp.zeros((1, 128), I32)
        for b in range(NS):
            offset = offset + jnp.where(meta_all[4 * x + k, 1:2, :] == b, meta_all[b, 0:1, :], 0)
        step = offset + 2044
        rows128 = iota((16, 128), 0)
        base_c, base_s = turn(((step * rows128) & (NIMG - 1)).astype(F32) * (1.0 / NIMG))
        for part in range(4):
            coarse_c, coarse_s = turn(((step * (16 * (rows128 + 16 * part))) & (NIMG - 1)).astype(F32) * (1.0 / NIMG))
            for q in range(16):
                cc, cs = coarse_c[q : q + 1], coarse_s[q : q + 1]
                at = part * 256 + q * 16
                ec[k, at : at + 16] = base_c * cc - base_s * cs
                es[k, at : at + 16] = -(base_s * cc + base_c * cs)

    def column_basis(k):
        half_steps(pos_all[4 * x + k, 1:2, :], ROWS, small)
        table_into(vb, (k,), BF16)

    def row_quarter(k):
        half_steps(pos_all[4 * x + k, 0:1, :], ROWS, small, 128.0 * lax.rem(z, 2).astype(F32))

        def put(at, lane_at, width, c, s):
            ub[k, pl.ds(at, 16), pl.ds(lane_at, width)] = jnp.where(z < 2, c, s)

        basis_into(small, lanes4, put, 8)

    def from_line(dz, e):
        arrived(0, dz, e)
        along_x(0, dz, e, 1)
        along_x(0, dz, e, -1)

    def across(dz):
        for e in range(2):
            for dx in (-1, 1):
                arrived(dx, dz, e)
                if e == (0 if dx == -1 else 1):
                    along_x(dx, dz, e, -dx)

    def transform(dx):
        line = lax.rem(x + dx % 4, 4)

        def modulate(i, carry):
            zz, cc = i // 2, lax.rem(i, 2)
            src = 4 * line + zz
            at = pl.multiple_of(src * 64 + cc * 32, 32)
            to = pl.multiple_of(i * 32, 32)
            re = qg[src, cc, :, 0:128].astype(F32)
            im = qg[src, cc, :, 128:256].astype(F32)
            for k in range(4):
                c, s = ec[k, pl.ds(at, 32)], es[k, pl.ds(at, 32)]
                qm[pl.ds(to, 32), k * 256 : k * 256 + 128] = (re * c - im * s).astype(BF16)
                qm[pl.ds(to, 32), k * 256 + 128 : k * 256 + 256] = (re * s + im * c).astype(BF16)
            return carry

        lax.fori_loop(0, 8, modulate, 0)
        lanes = pl.ds(pl.multiple_of(line * 256, 256), 256)
        for k in range(4):
            part = jnp.dot(bt[:, lanes], qm[:, k * 256 : k * 256 + 256], preferred_element_type=F32)
            if dx == 0:
                hacc[k] = part
            elif dx == 2:
                hs[k] = (hacc[k] + part).T.astype(BF16)
            else:
                hacc[k] += part

    column_phase(0)
    from_line(0, 1)
    column_phase(1)
    for dz in (-1, 1):
        for e in range(2):
            from_line(dz, e)
    column_phase(2)
    for e in range(2):
        from_line(2, e)
    column_phase(3)
    across(0)
    transform(0)
    column_basis(0)
    across(-1)
    column_basis(1)
    across(1)
    column_basis(2)
    across(2)
    column_basis(3)
    transform(-1)
    transform(1)
    for k in range(4):
        row_quarter(k)
    for dz in (0, -1, 1, 2):
        for e in range(2):
            arrived(2, dz, e)
    transform(2)

    part_copies = []
    for dz in (2, 1, -1, 0):
        k = lax.rem(z + dz % 4, 4)
        for at in range(0, ROWS, 256):
            lifted = jnp.dot(hs[k], vb[k, :, at : at + 256], preferred_element_type=F32)
            u = ub[k, :, at : at + 256]
            part_out[dz % 4, 0:1, at : at + 256] = jnp.sum(lifted[0:128] * u, axis=0, keepdims=True)
            part_out[dz % 4, 1:2, at : at + 256] = jnp.sum(lifted[128:256] * u, axis=0, keepdims=True)
        if dz:
            copy = pltpu.make_async_remote_copy(
                src_ref=part_out.at[dz % 4], dst_ref=part_in.at[-dz % 4],
                send_sem=d_send.at[dz % 4], recv_sem=d_recv.at[-dz % 4],
                device_id={"sub": place(0, dz)}, device_id_type=MESH,
            )
            copy.start()
            part_copies.append(copy)
    for copy in part_copies:
        copy.wait_recv()

    live_count = count[0]

    sums = part_out[0] + part_in[1] + part_in[2] + part_in[3]
    sum_re, sum_im = sums[0:1], sums[1:2]
    c, s = turn((pos[0, 0:1, :] + pos[0, 1:2, :]) * 0.5)
    scale = 4.0 / (M * FS)
    live = iota((1, ROWS), 1) < live_count
    re = obs[0, 0:1, :] - (sum_re * c + sum_im * s) * scale
    im = obs[0, 1:2, :] - (sum_im * c - sum_re * s) * scale
    both = jnp.concatenate([jnp.where(live, re, 0.0), jnp.where(live, im, 0.0)], axis=0)
    res_out[0] = both
    res_src[...] = both.astype(BF16)

    c_copies = []
    for d in range(1, NS):
        copy = pltpu.make_async_remote_copy(
            src_ref=res_src, dst_ref=res_all.at[j], send_sem=c_send.at[d - 1], recv_sem=c_recv.at[d - 1],
            device_id={"sub": lax.rem(j + d, NS)}, device_id_type=MESH,
        )
        copy.start()
        c_copies.append(copy)
    res_all[j] = res_src[...]

    rank = jnp.zeros((1, 128), F32)
    slots = [jnp.zeros((2, ROWS), F32) for _ in range(2)]
    for b in range(NS):
        match = jnp.where(meta_all[b, 1:2, :] == j, 1.0, 0.0)
        for slot in range(2):
            picked = jnp.where(rank == float(slot), match, 0.0)
            mask[slot, b : b + 1, :] = picked
            slots[slot] = slots[slot] + picked[:, 0:1] * pos_all[b]
        rank = rank + match
    for slot in range(2):
        slot_pos[slot] = slots[slot]
    for slot in range(2):
        half_steps(slot_pos[slot, 0:1, :], ROWS, small)
        table_into(ubo, (slot,), BF16)
        half_steps(slot_pos[slot, 1:2, :], ROWS, small)
        table_into(vbo, (slot,), F32)

    for copy in a_copies + m_copies + b_copies + part_copies:
        copy.wait_send()
    for copy in c_copies:
        copy.wait()

    rows = []
    for slot in range(2):
        r = jnp.zeros((2, ROWS), F32)
        for b in range(NS):
            r = r + mask[slot, b : b + 1, 0:1] * res_all[b].astype(F32)
        p = slot_pos[slot]
        c, s = turn((p[0:1, :] + p[1:2, :]) * 0.5)
        rows.append((r[0:1, :] * c - r[1:2, :] * s, r[0:1, :] * s + r[1:2, :] * c))
    for block in range(4):
        im, sine = block // 2, block % 2
        for slot in range(2):
            wb[block, :, slot * ROWS : slot * ROWS + ROWS] = (
                vbo[slot, sine * HALF : sine * HALF + HALF, :] * rows[slot][im]
            ).astype(BF16)
        for k in range(2):
            total[k, block] = sum(
                lax.dot_general(
                    ubo[slot, k * HALF : k * HALF + HALF, :], wb[block, :, slot * ROWS : slot * ROWS + ROWS],
                    (((1,), (1,)), ((), ())), preferred_element_type=F32,
                )
                for slot in range(2)
            )

    scale = 1.0 / math.sqrt(ROWS)
    flip = jnp.where(iota((HALF, HALF), 0) + iota((HALF, HALF), 1) == HALF - 1, 1.0, 0.0).astype(BF16)

    def flip_columns(a):
        return jnp.dot(a.astype(BF16), flip, preferred_element_type=F32)

    def flip_rows(a):
        return jnp.dot(flip, a, preferred_element_type=F32)

    for im in range(2):
        sign = 1.0 if im == 0 else -1.0
        cc, ss = total[0, 2 * im], total[1, 2 * im + 1]
        cs, sc = total[0, 3 - 2 * im], total[1, 2 - 2 * im]
        even, both = (cc - ss) * scale, (cc + ss) * scale
        y, w = (cs + sc) * (scale * sign), (cs - sc) * (scale * sign)
        left, right = slice(im * M, im * M + HALF), slice(im * M + HALF, im * M + M)
        grid_out[0, 0, HALF:M, right] = even + y
        grid_out[0, 0, HALF:M, left] = flip_columns(both - w)
        grid_out[0, 0, 0:HALF, right] = flip_rows((both + w).astype(BF16))
        grid_out[0, 0, 0:HALF, left] = flip_rows(flip_columns(even - y).astype(BF16))


def store(res_in, grid_in, res_out, grid_out, sem):
    copies = [
        pltpu.make_async_copy(res_in, res_out, sem.at[0]),
        pltpu.make_async_copy(grid_in, grid_out, sem.at[1]),
    ]
    for copy in copies:
        copy.start()
    for copy in copies:
        copy.wait()


def per_device(facets, tapers, row_offsets, col_offsets, block_subgrid, vis_count, positions, observed):
    vmem = pl.BlockSpec(memory_space=pltpu.VMEM)
    dma = pltpu.SemaphoreType.DMA
    residual, grid = pl.pallas_call(
        front,
        out_shape=(
            pltpu.VMEM((1, 2, ROWS), F32),
            pltpu.VMEM((1, 1, M, 2 * M), F32),
        ),
        in_specs=[pl.BlockSpec(memory_space=pltpu.HBM)] * 8,
        out_specs=(vmem, vmem),
        scratch_shapes=[
            pltpu.VMEM((2, FS), F32),
            pltpu.VMEM((1, 2, ROWS), F32),
            pltpu.VMEM((1, 2, ROWS), F32),
            pltpu.SMEM((NF,), I32),
            pltpu.SMEM((1,), I32),
            pltpu.SMEM((1, 1), I32),
            pltpu.SMEM((1,), I32),
            pltpu.VMEM((2, ROWS), BF16),
            pltpu.VMEM((NS, 2, ROWS), BF16),
            pltpu.VMEM((NS, 2, ROWS), F32),
            pltpu.VMEM((NS, 8, 128), I32),
            pltpu.VMEM((FS, 128), BF16),
            pltpu.VMEM((4, 32, FS), BF16),
            pltpu.VMEM((NF, 32, FS), BF16),
            pltpu.VMEM((M, FS), BF16),
            pltpu.VMEM((128, FS), BF16),
            pltpu.VMEM((2, 4, 32, 256), BF16),
            pltpu.VMEM((NS, 2, 32, 256), BF16),
            pltpu.VMEM((256, 1024), BF16),
            pltpu.VMEM((4, FS, 128), F32),
            pltpu.VMEM((4, FS, 128), F32),
            pltpu.VMEM((4, 128, ROWS), F32),
            pltpu.VMEM((4, M, ROWS), BF16),
            pltpu.VMEM((4, 256, M), BF16),
            pltpu.VMEM((4, M, 256), F32),
            pltpu.VMEM((4, 16, FS), F32),
            pltpu.VMEM((8, 128), I32),
            pltpu.VMEM((2, NS, 128), F32),
            pltpu.VMEM((2, 2, ROWS), F32),
            pltpu.VMEM((2, M, ROWS), BF16),
            pltpu.VMEM((2, M, ROWS), F32),
            pltpu.VMEM((4, HALF, 2 * ROWS), BF16),
            pltpu.VMEM((2, 4, HALF, HALF), F32),
            pltpu.VMEM((4, 2, ROWS), F32),
            pltpu.VMEM((4, 2, ROWS), F32),
            dma((8,)),
            dma((NF - 1,)), dma((8,)),
            dma((4,)), dma((4,)),
            dma((32,)), dma((32,)),
            dma((NS - 1,)), dma((NS - 1,)),
            dma((NS - 1,)), dma((NS - 1,)),
            dma((NS - 1,)), dma((NS - 1,)),
        ],
        compiler_params=pltpu.CompilerParams(collective_id=0, has_side_effects=True),
        name="front",
    )(facets, tapers, row_offsets, col_offsets, block_subgrid, vis_count, positions, observed)
    hbm = pl.BlockSpec(memory_space=pltpu.HBM)
    return pl.pallas_call(
        store,
        out_shape=(
            jax.ShapeDtypeStruct((1, 2, ROWS), F32),
            jax.ShapeDtypeStruct((1, 1, M, 2 * M), F32),
        ),
        in_specs=[vmem, vmem],
        out_specs=(hbm, hbm),
        scratch_shapes=[pltpu.SemaphoreType.DMA((2,))],
        name="widen",
    )(pltpu.with_memory_space_constraint(residual, pltpu.VMEM), pltpu.with_memory_space_constraint(grid, pltpu.VMEM))


def solution(mesh):
    in_specs = (
        P("facet", None, None),
        P(),
        P(),
        P("sub"),
        P(("facet", "sub"), None),
        P(("facet", "sub")),
        P(("facet", "sub"), None, None),
        P(("facet", "sub"), None, None),
    )
    out_specs = (P(("facet", "sub"), None, None), P("facet", "sub", None, None))
    return jax.shard_map(per_device, mesh=mesh, in_specs=in_specs, out_specs=out_specs, check_vma=False)
```

```python
import functools
import math

import jax
import jax.numpy as jnp
from jax import lax
from jax.experimental import pallas as pl
from jax.experimental.pallas import tpu as pltpu
from jax.sharding import PartitionSpec as P

M = 512
HALF = 256
FS = 1024
NIMG = 8192
ROWS = 1024
NF = 8
NS = 16
MESH = pl.DeviceIdType.MESH
F32 = jnp.float32
BF16 = jnp.bfloat16
I32 = jnp.int32


def turn(t):
    u = (t - jnp.round(t)) * math.pi
    v = u * u
    s = 1.0 / 6227020800.0
    for c in (-1.0 / 39916800.0, 1.0 / 362880.0, -1.0 / 5040.0, 1.0 / 120.0, -1.0 / 6.0, 1.0):
        s = s * v + c
    s = s * u
    k = 1.0 / 479001600.0
    for c in (-1.0 / 3628800.0, 1.0 / 40320.0, -1.0 / 720.0, 1.0 / 24.0, -0.5, 1.0):
        k = k * v + c
    return 1.0 - 2.0 * s * s, 2.0 * s * k


def grow(base, coarse, steps, put):
    bc, bs = base

    def step(q, carry):
        cc, cs = coarse(q)
        put(q, bc * cc - bs * cs, bs * cc + bc * cs)
        return carry

    lax.fori_loop(0, steps, step, 0)


def iota(shape, dim):
    return lax.broadcasted_iota(I32, shape, dim)


def half_steps(p, n, m_ref, start=0.0):
    shape = (16, n)
    rows = iota(shape, 0).astype(F32)
    m_ref[0], m_ref[1] = turn(p * (rows + 0.5))
    m_ref[2], m_ref[3] = turn(p * (rows * 16.0 + start))


def basis_into(m_ref, lanes, put, steps=16):
    for at, width in lanes:
        base = (m_ref[0, :, pl.ds(at, width)], m_ref[1, :, pl.ds(at, width)])

        def coarse(q, at=at, width=width):
            return m_ref[2, pl.ds(q, 1), pl.ds(at, width)], m_ref[3, pl.ds(q, 1), pl.ds(at, width)]

        def put_here(q, c, s, at=at, width=width):
            put(pl.multiple_of(q * 16, 16), at, width, c, s)

        grow(base, coarse, steps, put_here)


def front(
    facets, taper_in, row_off_in, col_off_in, target_in, count_in, pos_in, obs_in,
    res_out, grid_out,
    tapers, pos, obs, row_off, col_off, target, count, res_src,
    res_all, pos_all, meta_all, fac, tt, facs, bt, zs, uq, qg, qm, ec, es, ub, vb, hs, hacc, small, meta_src,
    mask, slot_pos, ubo, vbo, wb, total, part_out, part_in,
    load_sem, a_send, a_recv, d_send, d_recv, b_send, b_recv, m_send, m_recv, p_send, p_recv, c_send, c_recv,
):
    f = lax.axis_index("facet")
    j = lax.axis_index("sub")
    core = lax.rem(f, 2)
    x, z = j // 4, lax.rem(j, 4)
    pair, odd = j // 2, lax.rem(j, 2)
    at128 = pl.multiple_of(pair * 128, 128)

    y = f // 2
    barrier = pltpu.get_barrier_semaphore()
    near = [2 * lax.rem(y + dy, 4) + c for dy in (1, 3) for c in range(2)] + [f + 1 - 2 * core]
    for peer in near:
        pl.semaphore_signal(barrier, inc=1, device_id={"facet": peer}, device_id_type=MESH)
    for d in range(1, NS):
        pl.semaphore_signal(barrier, inc=1, device_id={"sub": lax.rem(j + d, NS)}, device_id_type=MESH)
    for dz in range(1, 4):
        other = {"facet": f + 1 - 2 * core, "sub": 4 * x + lax.rem(z + dz, 4)}
        pl.semaphore_signal(barrier, inc=1, device_id=other, device_id_type=MESH)
    loads = [
        pltpu.make_async_copy(src, dst, load_sem.at[i])
        for i, (src, dst) in enumerate((
            (facets.at[0, :, pl.ds(at128, 128)], fac), (taper_in, tapers), (pos_in, pos), (obs_in, obs),
            (row_off_in, row_off), (col_off_in, col_off), (target_in, target), (count_in, count),
        ))
    ]
    for load in loads:
        load.start()
    for load in loads:
        load.wait()

    rows8 = iota((8, 128), 0)
    meta_src[...] = jnp.where(rows8 == 0, col_off[0], jnp.where(rows8 == 1, target[0, 0], count[0]))
    meta_all[j] = meta_src[...]
    pos_all[j] = pos[0]

    by_column = fac[...].astype(F32) * tapers[1:2, pl.ds(at128, 128)]
    turned = (by_column.T * tapers[0:1, :]).astype(BF16)
    for g in range(4):
        tt[g] = turned[g * 32 : g * 32 + 32]
    facs[f] = tt[2 * odd + core]

    pl.semaphore_wait(barrier, 5 + NS - 1 + 3)
    a_copies, m_copies = [], []

    def facet_at(dy, c):
        return 2 * lax.rem(y + dy % 4, 4) + c

    def send_slice(src, source, dy, c, slot, h):
        at = pl.ds(16 * h, 16)
        copy = pltpu.make_async_remote_copy(
            src_ref=src.at[at], dst_ref=facs.at[source, at],
            send_sem=a_send.at[len(a_copies)], recv_sem=a_recv.at[slot, h],
            device_id={"facet": facet_at(dy, c)}, device_id_type=MESH,
        )
        copy.start()
        a_copies.append(copy)

    def slice_arrived(dy, c, slot, h):
        ref = facs.at[facet_at(dy, c), pl.ds(16 * h, 16)]
        pltpu.make_async_remote_copy(
            src_ref=ref, dst_ref=ref, send_sem=a_send.at[0], recv_sem=a_recv.at[slot, h],
            device_id={"facet": f}, device_id_type=MESH,
        ).wait_recv()

    for h in range(2):
        for dy in (1, 3):
            for c in range(2):
                send_slice(tt.at[2 * odd + c], f, dy, c, 2 * (4 - dy) + core, h)
    for h in range(2):
        send_slice(tt.at[2 * odd + 1 - core], f, 0, 1 - core, 0, h)
    for d in range(1, NS):
        peer = lax.rem(j + d, NS)
        for src, dst, ss, rs in ((meta_src, meta_all, m_send, m_recv), (pos.at[0], pos_all, p_send, p_recv)):
            copy = pltpu.make_async_remote_copy(
                src_ref=src, dst_ref=dst.at[j], send_sem=ss.at[d - 1], recv_sem=rs.at[d - 1],
                device_id={"sub": peer}, device_id_type=MESH,
            )
            copy.start()
            m_copies.append(copy)

    lanes4 = [(0, 256), (256, 256), (512, 256), (768, 256)]

    def table_into(ref, lead, dtype):
        def put(at, lane_at, width, c, s):
            ref[(*lead, pl.ds(at, 16), pl.ds(lane_at, width))] = c.astype(dtype)
            ref[(*lead, pl.ds(at + HALF, 16), pl.ds(lane_at, width))] = s.astype(dtype)

        basis_into(small, lanes4, put)

    def relay_slices():
        for h in range(2):
            slice_arrived(3, 0, 6, h)
            send_slice(facs.at[facet_at(3, 0)], facet_at(3, 0), 1, core, 4, h)
            slice_arrived(1, 1, 3, h)
            send_slice(facs.at[facet_at(1, 1)], facet_at(1, 1), 3, core, 5, h)

    lane = iota((16, FS), 1)
    row = iota((16, FS), 0)
    small[0], small[1] = turn((((2 * row + 1) * lane) & 2047).astype(F32) * (1.0 / 2048))
    small[2], small[3] = turn(((32 * row * lane) & 2047).astype(F32) * (1.0 / 2048))
    relay_slices()
    table_into(bt, (), BF16)

    phases = []
    rows_f = iota((NF, FS), 0)
    lane_f = iota((NF, FS), 1)
    for aa in range(2):
        off = row_off[2 * (f // 2) + aa]
        r = (off * (rows_f * FS + lane_f) + 2044 * lane_f) & (NIMG - 1)
        c, s = turn(r.astype(F32) * (1.0 / NIMG))
        phases.append((c, -s))

    def column_phase(k):
        offset = jnp.zeros((1, 128), I32)
        for b in range(NS):
            offset = offset + jnp.where(meta_all[4 * x + k, 1:2, :] == b, meta_all[b, 0:1, :], 0)
        step = offset + 2044
        rows128 = iota((16, 128), 0)
        base_c, base_s = turn(((step * rows128) & (NIMG - 1)).astype(F32) * (1.0 / NIMG))
        for part in range(4):
            coarse_c, coarse_s = turn(((step * (16 * (rows128 + 16 * part))) & (NIMG - 1)).astype(F32) * (1.0 / NIMG))
            for q in range(16):
                cc, cs = coarse_c[q : q + 1], coarse_s[q : q + 1]
                at = part * 256 + q * 16
                ec[k, at : at + 16] = base_c * cc - base_s * cs
                es[k, at : at + 16] = -(base_s * cc + base_c * cs)

    def column_basis(k):
        half_steps(pos_all[4 * x + k, 1:2, :], ROWS, small)
        table_into(vb, (k,), BF16)

    def row_quarter(k):
        half_steps(pos_all[4 * x + k, 0:1, :], ROWS, small, 128.0 * lax.rem(z, 2).astype(F32))

        def put(at, lane_at, width, c, s):
            ub[k, pl.ds(at, 16), pl.ds(lane_at, width)] = jnp.where(z < 2, c, s)

        basis_into(small, lanes4, put, 8)

    column_basis(z)
    row_quarter(z)
    def slot_table(slot, k):
        half_steps(slot_pos[slot, k : k + 1, :], ROWS, small)
        table_into(ubo if k == 0 else vbo, (slot,), BF16 if k == 0 else F32)

    def other(i):
        return lax.rem(z + i, 4)

    for dy, c, slot in ((0, 1 - core, 0), (3, 1, 7), (1, 0, 2), (2, 0, 4), (2, 1, 5)):
        for h in range(2):
            slice_arrived(dy, c, slot, h)
    for at, width in lanes4:
        sums = [jnp.zeros((32, width), F32) for _ in range(4)]
        for g in range(NF):
            t = facs[g, :, at : at + width].astype(F32)
            for aa in range(2):
                sums[2 * aa] = sums[2 * aa] + t * phases[aa][0][g : g + 1, at : at + width]
                sums[2 * aa + 1] = sums[2 * aa + 1] + t * phases[aa][1][g : g + 1, at : at + width]
        for i in range(4):
            zs[i * 32 : i * 32 + 32, at : at + width] = sums[i].astype(BF16)
    turned_rows = lax.dot_general(
        zs[...], bt[...], (((1,), (1,)), ((), ())), preferred_element_type=F32
    ).astype(BF16)
    for aa in range(2):
        for k in range(4):
            uq[aa, k] = jnp.concatenate([
                turned_rows[aa * 64 : aa * 64 + 32, k * 128 : k * 128 + 128],
                turned_rows[aa * 64 + 32 : aa * 64 + 64, k * 128 : k * 128 + 128],
            ], axis=1)
    qg[j, core] = uq[core, z]

    def place(dx, dz):
        return 4 * lax.rem(x + dx % 4, 4) + lax.rem(z + dz % 4, 4)

    def core_of(e):
        return core if e == 0 else 1 - core

    b_copies = []

    def send_unit(src, dst, slot, device):
        copy = pltpu.make_async_remote_copy(
            src_ref=src, dst_ref=dst, send_sem=b_send.at[len(b_copies)], recv_sem=b_recv.at[slot],
            device_id=device, device_id_type=MESH,
        )
        copy.start()
        b_copies.append(copy)

    def slot_of(dx, dz, e):
        return ((dx % 4) * 4 + dz % 4) * 2 + e

    def unit(dx, dz, e):
        return qg.at[place(dx, dz), core_of(e)]

    def along_x(dx, dz, e, ex):
        send_unit(unit(dx, dz, e), unit(dx, dz, e), slot_of(dx - ex, dz, e), {"sub": place(ex, 0)})

    def arrived(dx, dz, e):
        pltpu.make_async_remote_copy(
            src_ref=unit(dx, dz, e), dst_ref=unit(dx, dz, e), send_sem=b_send.at[0],
            recv_sem=b_recv.at[slot_of(dx, dz, e)], device_id={"sub": j}, device_id_type=MESH,
        ).wait_recv()

    for dz in (2, 1, -1, 0):
        for e in range(2):
            if dz or e:
                send_unit(
                    uq.at[core_of(e), lax.rem(z + dz % 4, 4)], qg.at[j, core], slot_of(0, -dz, e),
                    {"facet": 2 * y + core_of(e), "sub": place(0, dz)},
                )
    along_x(0, 0, 0, 1)
    along_x(0, 0, 0, -1)

    for copy in m_copies:
        copy.wait_recv()

    rank = jnp.zeros((1, 128), F32)
    slots = [jnp.zeros((2, ROWS), F32) for _ in range(2)]
    for b in range(NS):
        match = jnp.where(meta_all[b, 1:2, :] == j, 1.0, 0.0)
        for slot in range(2):
            picked = jnp.where(rank == float(slot), match, 0.0)
            mask[slot, b : b + 1, :] = picked
            slots[slot] = slots[slot] + picked[:, 0:1] * pos_all[b]
        rank = rank + match
    for slot in range(2):
        slot_pos[slot] = slots[slot]
    column_phase(z)

    def from_line(dz, e):
        arrived(0, dz, e)
        along_x(0, dz, e, 1)
        along_x(0, dz, e, -1)

    def across(dz):
        for e in range(2):
            for dx in (-1, 1):
                arrived(dx, dz, e)
                if e == (0 if dx == -1 else 1):
                    along_x(dx, dz, e, -dx)

    def transform(dx):
        line = lax.rem(x + dx % 4, 4)

        def modulate(i, carry):
            zz, cc = i // 2, lax.rem(i, 2)
            src = 4 * line + zz
            at = pl.multiple_of(src * 64 + cc * 32, 32)
            to = pl.multiple_of(i * 32, 32)
            re = qg[src, cc, :, 0:128].astype(F32)
            im = qg[src, cc, :, 128:256].astype(F32)
            for k in range(4):
                c, s = ec[k, pl.ds(at, 32)], es[k, pl.ds(at, 32)]
                qm[pl.ds(to, 32), k * 256 : k * 256 + 128] = (re * c - im * s).astype(BF16)
                qm[pl.ds(to, 32), k * 256 + 128 : k * 256 + 256] = (re * s + im * c).astype(BF16)
            return carry

        lax.fori_loop(0, 8, modulate, 0)
        lanes = pl.ds(pl.multiple_of(line * 256, 256), 256)
        for k in range(4):
            part = jnp.dot(bt[:, lanes], qm[:, k * 256 : k * 256 + 256], preferred_element_type=F32)
            if dx == 0:
                hacc[k] = part
            elif dx == 2:
                hs[k] = (hacc[k] + part).T.astype(BF16)
            else:
                hacc[k] += part

    from_line(0, 1)
    column_phase(other(1))
    for dz in (-1, 1):
        for e in range(2):
            from_line(dz, e)
    column_phase(other(2))
    for e in range(2):
        from_line(2, e)
    column_phase(other(3))
    across(0)
    transform(0)
    column_basis(other(1))
    across(-1)
    column_basis(other(2))
    across(1)
    column_basis(other(3))
    across(2)
    row_quarter(other(1))
    transform(-1)
    transform(1)
    row_quarter(other(2))
    row_quarter(other(3))
    for dz in (0, -1, 1, 2):
        for e in range(2):
            arrived(2, dz, e)
    transform(2)

    part_copies = []
    for dz in (2, 1, -1, 0):
        k = lax.rem(z + dz % 4, 4)
        for at in range(0, ROWS, 256):
            lifted = jnp.dot(hs[k], vb[k, :, at : at + 256], preferred_element_type=F32)
            u = ub[k, :, at : at + 256]
            part_out[dz % 4, 0:1, at : at + 256] = jnp.sum(lifted[0:128] * u, axis=0, keepdims=True)
            part_out[dz % 4, 1:2, at : at + 256] = jnp.sum(lifted[128:256] * u, axis=0, keepdims=True)
        if dz:
            copy = pltpu.make_async_remote_copy(
                src_ref=part_out.at[dz % 4], dst_ref=part_in.at[-dz % 4],
                send_sem=d_send.at[dz % 4], recv_sem=d_recv.at[-dz % 4],
                device_id={"sub": place(0, dz)}, device_id_type=MESH,
            )
            copy.start()
            part_copies.append(copy)
    for copy in part_copies:
        copy.wait_recv()

    live_count = count[0]

    sums = part_out[0] + part_in[1] + part_in[2] + part_in[3]
    sum_re, sum_im = sums[0:1], sums[1:2]
    c, s = turn((pos[0, 0:1, :] + pos[0, 1:2, :]) * 0.5)
    scale = 4.0 / (M * FS)
    live = iota((1, ROWS), 1) < live_count
    re = obs[0, 0:1, :] - (sum_re * c + sum_im * s) * scale
    im = obs[0, 1:2, :] - (sum_im * c - sum_re * s) * scale
    both = jnp.concatenate([jnp.where(live, re, 0.0), jnp.where(live, im, 0.0)], axis=0)
    res_out[0] = both
    res_src[...] = both.astype(BF16)

    c_copies = []
    for d in range(1, NS):
        copy = pltpu.make_async_remote_copy(
            src_ref=res_src, dst_ref=res_all.at[j], send_sem=c_send.at[d - 1], recv_sem=c_recv.at[d - 1],
            device_id={"sub": lax.rem(j + d, NS)}, device_id_type=MESH,
        )
        copy.start()
        c_copies.append(copy)
    res_all[j] = res_src[...]

    slot_table(0, 0)
    slot_table(0, 1)
    slot_table(1, 0)
    slot_table(1, 1)

    for copy in a_copies + m_copies + b_copies + part_copies:
        copy.wait_send()
    for copy in c_copies:
        copy.wait()

    rows = []
    for slot in range(2):
        r = jnp.zeros((2, ROWS), F32)
        for b in range(NS):
            r = r + mask[slot, b : b + 1, 0:1] * res_all[b].astype(F32)
        p = slot_pos[slot]
        c, s = turn((p[0:1, :] + p[1:2, :]) * 0.5)
        rows.append((r[0:1, :] * c - r[1:2, :] * s, r[0:1, :] * s + r[1:2, :] * c))
    for block in range(4):
        im, sine = block // 2, block % 2
        for slot in range(2):
            wb[block, :, slot * ROWS : slot * ROWS + ROWS] = (
                vbo[slot, sine * HALF : sine * HALF + HALF, :] * rows[slot][im]
            ).astype(BF16)
        product = sum(
            lax.dot_general(
                ubo[slot], wb[block, :, slot * ROWS : slot * ROWS + ROWS],
                (((1,), (1,)), ((), ())), preferred_element_type=F32,
            )
            for slot in range(2)
        )
        total[0, block] = product[0:HALF]
        total[1, block] = product[HALF:M]

    scale = 1.0 / math.sqrt(ROWS)
    flip = jnp.where(iota((HALF, HALF), 0) + iota((HALF, HALF), 1) == HALF - 1, 1.0, 0.0).astype(BF16)

    def flip_columns(a):
        return jnp.dot(a.astype(BF16), flip, preferred_element_type=F32)

    def flip_rows(a):
        return jnp.dot(flip, a, preferred_element_type=F32)

    for im in range(2):
        sign = 1.0 if im == 0 else -1.0
        cc, ss = total[0, 2 * im], total[1, 2 * im + 1]
        cs, sc = total[0, 3 - 2 * im], total[1, 2 - 2 * im]
        even, both = (cc - ss) * scale, (cc + ss) * scale
        y, w = (cs + sc) * (scale * sign), (cs - sc) * (scale * sign)
        left, right = slice(im * M, im * M + HALF), slice(im * M + HALF, im * M + M)
        grid_out[0, 0, HALF:M, right] = even + y
        grid_out[0, 0, HALF:M, left] = flip_columns(both - w)
        grid_out[0, 0, 0:HALF, right] = flip_rows((both + w).astype(BF16))
        grid_out[0, 0, 0:HALF, left] = flip_rows(flip_columns(even - y).astype(BF16))


def store(res_in, grid_in, res_out, grid_out, sem):
    copies = [
        pltpu.make_async_copy(res_in, res_out, sem.at[0]),
        pltpu.make_async_copy(grid_in, grid_out, sem.at[1]),
    ]
    for copy in copies:
        copy.start()
    for copy in copies:
        copy.wait()


def per_device(facets, tapers, row_offsets, col_offsets, block_subgrid, vis_count, positions, observed):
    vmem = pl.BlockSpec(memory_space=pltpu.VMEM)
    dma = pltpu.SemaphoreType.DMA
    residual, grid = pl.pallas_call(
        front,
        out_shape=(
            pltpu.VMEM((1, 2, ROWS), F32),
            pltpu.VMEM((1, 1, M, 2 * M), F32),
        ),
        in_specs=[pl.BlockSpec(memory_space=pltpu.HBM)] * 8,
        out_specs=(vmem, vmem),
        scratch_shapes=[
            pltpu.VMEM((2, FS), F32),
            pltpu.VMEM((1, 2, ROWS), F32),
            pltpu.VMEM((1, 2, ROWS), F32),
            pltpu.SMEM((NF,), I32),
            pltpu.SMEM((1,), I32),
            pltpu.SMEM((1, 1), I32),
            pltpu.SMEM((1,), I32),
            pltpu.VMEM((2, ROWS), BF16),
            pltpu.VMEM((NS, 2, ROWS), BF16),
            pltpu.VMEM((NS, 2, ROWS), F32),
            pltpu.VMEM((NS, 8, 128), I32),
            pltpu.VMEM((FS, 128), BF16),
            pltpu.VMEM((4, 32, FS), BF16),
            pltpu.VMEM((NF, 32, FS), BF16),
            pltpu.VMEM((M, FS), BF16),
            pltpu.VMEM((128, FS), BF16),
            pltpu.VMEM((2, 4, 32, 256), BF16),
            pltpu.VMEM((NS, 2, 32, 256), BF16),
            pltpu.VMEM((256, 1024), BF16),
            pltpu.VMEM((4, FS, 128), F32),
            pltpu.VMEM((4, FS, 128), F32),
            pltpu.VMEM((4, 128, ROWS), F32),
            pltpu.VMEM((4, M, ROWS), BF16),
            pltpu.VMEM((4, 256, M), BF16),
            pltpu.VMEM((4, M, 256), F32),
            pltpu.VMEM((4, 16, FS), F32),
            pltpu.VMEM((8, 128), I32),
            pltpu.VMEM((2, NS, 128), F32),
            pltpu.VMEM((2, 2, ROWS), F32),
            pltpu.VMEM((2, M, ROWS), BF16),
            pltpu.VMEM((2, M, ROWS), F32),
            pltpu.VMEM((4, HALF, 2 * ROWS), BF16),
            pltpu.VMEM((2, 4, HALF, HALF), F32),
            pltpu.VMEM((4, 2, ROWS), F32),
            pltpu.VMEM((4, 2, ROWS), F32),
            dma((8,)),
            dma((14,)), dma((8, 2)),
            dma((4,)), dma((4,)),
            dma((32,)), dma((32,)),
            dma((NS - 1,)), dma((NS - 1,)),
            dma((NS - 1,)), dma((NS - 1,)),
            dma((NS - 1,)), dma((NS - 1,)),
        ],
        compiler_params=pltpu.CompilerParams(collective_id=0, has_side_effects=True),
        name="front",
    )(facets, tapers, row_offsets, col_offsets, block_subgrid, vis_count, positions, observed)
    hbm = pl.BlockSpec(memory_space=pltpu.HBM)
    return pl.pallas_call(
        store,
        out_shape=(
            jax.ShapeDtypeStruct((1, 2, ROWS), F32),
            jax.ShapeDtypeStruct((1, 1, M, 2 * M), F32),
        ),
        in_specs=[vmem, vmem],
        out_specs=(hbm, hbm),
        scratch_shapes=[pltpu.SemaphoreType.DMA((2,))],
        name="widen",
    )(pltpu.with_memory_space_constraint(residual, pltpu.VMEM), pltpu.with_memory_space_constraint(grid, pltpu.VMEM))


def solution(mesh):
    in_specs = (
        P("facet", None, None),
        P(),
        P(),
        P("sub"),
        P(("facet", "sub"), None),
        P(("facet", "sub")),
        P(("facet", "sub"), None, None),
        P(("facet", "sub"), None, None),
    )
    out_specs = (P(("facet", "sub"), None, None), P("facet", "sub", None, None))
    return jax.shard_map(per_device, mesh=mesh, in_specs=in_specs, out_specs=out_specs, check_vma=False)
```
